32 devices in a mesh: wide: 8 (over z, y), narrow: 4 (over x, core).
Axes of the slice: x: 2, y: 2, z: 4, core: 2. Of those that a mesh axis runs over, the one named last changes fastest.
Arguments:
- inputs: bfloat16 [16384, 1024], P('wide', 'narrow'), may hold values from -6 to 6
- lengths: int32 [16], P('wide'), may hold values from 256 to 1024, as said below
- attn_gain: float32 [1024], replicated, may hold values from 0.25 to 1.75
- attn_in_weight: bfloat16 [3, 1024, 1024], P(None, 'wide', 'narrow'), may hold values from -0.1875 to 0.1875
- attn_out_weight: bfloat16 [1024, 1024], P('narrow', 'wide'), may hold values from -3 to 3
- mlp_gain: float32 [1024], replicated, may hold values from 0.25 to 1.75
- mlp_in_weight: bfloat16 [2, 1024, 2624], P(None, 'wide', 'narrow'), may hold values from -0.1875 to 0.1875
- mlp_out_weight: bfloat16 [2624, 1024], P('narrow', 'wide'), may hold values from -0.125 to 0.125
- cotangent: bfloat16 [16384, 1024], P('wide', 'narrow'), may hold values from -6 to 6
Outputs:
- output: float32 [16384, 1024], P('wide', 'narrow')
- inputs_grad: float32 [16384, 1024], P('wide', 'narrow')
- attn_gain_grad: float32 [1024], P('narrow')
- attn_in_grad: float32 [3, 1024, 1024], P(None, 'wide', 'narrow')
- attn_out_grad: float32 [1024, 1024], P('narrow', 'wide')
- mlp_gain_grad: float32 [1024], P('narrow')
- mlp_in_grad: float32 [2, 1024, 2624], P(None, 'wide', 'narrow')
- mlp_out_grad: float32 [2624, 1024], P('narrow', 'wide')
The draws below stay inside these ranges and needn't reach their ends.
Inputs may be any that keep to these rules, and one draw needn't show every extreme that they name: `lengths`: each sequence's live slots; its slots from there on are padding; some sequence has all 1024 live.
All inputs are finite; a program needn't handle non-finite values.
Results may differ from the reference program's by a relative error of at most 0.02.
Values may be sent and summed in bfloat16 or wider, within the bound.
No kernel may reach another device: no remote copies, remote signals or barrier semaphores. Data moves between devices by JAX's collectives and lax.ppermute only.
A program may use at most 128 MiB of HBM per device.

```python
import jax
import jax.numpy as jnp
from jax import lax

D = 1024
HEADS = 16
HEAD_DIM = 64
FF = 2624
SLOTS = 1024
SEQ_DEV = 2
SEQS = 16
TOKENS = 16384


def draw_lengths(key, part):
    first_key, second_key = jax.random.split(key)
    drawn = jax.random.randint(first_key, (SEQS,), SLOTS // 4, SLOTS + 1)
    full_at = jax.random.randint(second_key, (), 0, SEQS)
    return jnp.where(jnp.arange(SEQS) == full_at, SLOTS, drawn).astype(jnp.int32)


def level_of(stream_key, dims, cuts, least, largest):
    gain = 1.0
    for position, shards_of in cuts:
        heights = jax.random.uniform(jax.random.fold_in(jax.random.fold_in(stream_key, 6), position), (shards_of,), jnp.float32, least / len(cuts), largest / len(cuts))
        gain = gain * jnp.repeat(jnp.exp(heights), dims[position] // shards_of).reshape((-1,) + (1,) * (len(dims) - 1 - position))
    return gain


def gaussian(rng, dims, width, limit, shards=(), held_as=jnp.bfloat16):
    loudness = level_of(rng, dims, shards, -0.22, 0.18) if shards else 1.0
    values = jax.random.normal(rng, dims, jnp.float32) * width * loudness
    return jnp.minimum(jnp.maximum(values, -limit), limit).astype(held_as)


def setup_inputs(seed: int = 0) -> dict:
    key_of = jax.random.split(jax.random.key(seed), 10)
    return {
        "inputs": gaussian(key_of[0], (TOKENS, D), 1.0, 6.0, ((0, 8), (1, 4))),
        "lengths": draw_lengths(jax.random.fold_in(key_of[9], 71), 0),
        "attn_gain": jnp.clip(1.0 + 0.15 * jax.random.normal(key_of[2], (D,), jnp.float32), 0.25, 1.75),
        "attn_in_weight": gaussian(key_of[3], (3, D, D), D ** -0.5, 0.1875, ((1, 8), (2, 4))),
        "attn_out_weight": gaussian(key_of[4], (D, D), (D * 4 // SLOTS) ** -0.5, 3.0, ((0, 4), (1, 8))),
        "mlp_gain": jnp.clip(1.0 + 0.15 * jax.random.normal(key_of[5], (D,), jnp.float32), 0.25, 1.75),
        "mlp_in_weight": gaussian(key_of[6], (2, D, FF), D ** -0.5, 0.1875, ((1, 8), (2, 4))),
        "mlp_out_weight": gaussian(key_of[7], (FF, D), FF ** -0.5, 0.125, ((0, 4), (1, 8))),
        "cotangent": gaussian(key_of[8], (TOKENS, D), 1.0, 6.0, ((0, 8), (1, 4))),
    }


@jax.custom_vjp
def low(v):
    return lax.optimization_barrier(v.astype(jnp.bfloat16)).astype(jnp.float32)

@jax.custom_vjp
def low_back(v):
    return v

def low_keep(v):
    return (low(v), None)

def low_pass(kept, grad):
    return (grad,)

def back_keep(v):
    return (v, None)

def back_low(kept, grad):
    return (low(grad),)
low.defvjp(low_keep, low_pass)
low_back.defvjp(back_keep, back_low)
epsilon = 1e-05
theta_base = 160000.0
masked_score = -1e+30
high = lax.Precision.HIGHEST

def normalize(rows):
    center = rows - lax.optimization_barrier(jnp.mean(rows, axis=-1, keepdims=True))
    factor = lax.rsqrt(lax.optimization_barrier(jnp.mean(center * center, axis=-1, keepdims=True)) + epsilon)
    return center * factor

def rotary_tables():
    half_dim = HEAD_DIM // 2
    inverse = theta_base ** (-2.0 * jnp.arange(half_dim, dtype=jnp.float32) / HEAD_DIM)
    angles = jnp.arange(SLOTS, dtype=jnp.float32)[:, None] * inverse[None, :]
    return (jnp.cos(angles)[None, :, None, :], jnp.sin(angles)[None, :, None, :])

def rotate(values, cos_table, sin_table):
    half_dim = values.shape[-1] // 2
    leading = values[..., :half_dim]
    trailing = values[..., half_dim:]
    return jnp.concatenate([leading * cos_table - trailing * sin_table, trailing * cos_table + leading * sin_table], axis=-1)

def attend(operands):
    query_seq, key_seq, value_seq, length = operands
    keep_keys = jnp.arange(SLOTS) < length
    scores = low_back(jnp.einsum('qhd,khd->hqk', query_seq, key_seq, precision=high) * HEAD_DIM ** (-0.5))
    scores = jnp.where(keep_keys[None, None, :], scores, masked_score)
    attention = low(jax.nn.softmax(scores, axis=-1))
    return jnp.einsum('hqk,khd->qhd', attention, value_seq, precision=high)

def layer(rows, weights, block_lengths):
    attn_gain, attn_in_weight, attn_out_weight, mlp_gain, mlp_in_weight, mlp_out_weight = weights
    group_size = rows.shape[0]
    cos_table, sin_table = rotary_tables()
    normed_one = low(normalize(rows) * attn_gain)
    projected = low_back(jnp.einsum('gsd,kdc->kgsc', normed_one, attn_in_weight, precision=high))
    head_shape = (group_size, SLOTS, HEADS, HEAD_DIM)
    queries = low(rotate(projected[0].reshape(head_shape), cos_table, sin_table))
    keys = low(rotate(projected[1].reshape(head_shape), cos_table, sin_table))
    values = low(projected[2].reshape(head_shape))
    attended = lax.map(jax.checkpoint(attend), (queries, keys, values, block_lengths))
    attended = low(low_back(attended.reshape(group_size, SLOTS, D)))
    residual = rows + low_back(jnp.einsum('gsc,cd->gsd', attended, attn_out_weight, precision=high))
    normed_two = low(normalize(residual) * mlp_gain)
    expanded = low_back(jnp.einsum('gsd,kdf->kgsf', normed_two, mlp_in_weight, precision=high))
    mixed = low(jax.nn.gelu(expanded[0], approximate=False) * expanded[1])
    branch = low_back(jnp.einsum('gsf,fd->gsd', mixed, mlp_out_weight, precision=high))
    keep_rows = (jnp.arange(SLOTS)[None, :] < block_lengths[:, None]).astype(rows.dtype)
    return (residual + branch) * keep_rows[..., None]

def reference(inputs, lengths, attn_gain, attn_in_weight, attn_out_weight, mlp_gain, mlp_in_weight, mlp_out_weight, cotangent):
    weights_full = tuple((value.astype(jnp.float32) for value in (attn_gain, attn_in_weight, attn_out_weight, mlp_gain, mlp_in_weight, mlp_out_weight)))
    group_count = SEQS // SEQ_DEV
    rows_all = inputs.astype(jnp.float32).reshape(group_count, SEQ_DEV, SLOTS, D)
    cot_all = cotangent.astype(jnp.float32).reshape(group_count, SEQ_DEV, SLOTS, D)
    length_all = lengths.reshape(group_count, SEQ_DEV)

    def group_step(totals, operands):
        block_rows, block_cot, block_lengths = operands
        result, pullback = jax.vjp(lambda rows, weights: layer(rows, weights, block_lengths), block_rows, weights_full)
        rows_grad, weight_grad = pullback(block_cot)
        totals = jax.tree.map(lambda left, right: left + right, totals, weight_grad)
        return (totals, (result, rows_grad))
    zero_grads = jax.tree.map(jnp.zeros_like, weights_full)
    totals, (results, rows_grads) = lax.scan(group_step, zero_grads, (rows_all, cot_all, length_all))
    return (results.reshape(SEQS * SLOTS, D), rows_grads.reshape(SEQS * SLOTS, D), totals[0], totals[1], totals[2], totals[3], totals[4], totals[5])
```

```python
import functools

import jax
import jax.numpy as jnp
from jax import lax
from jax.experimental import pallas as pl
from jax.experimental.pallas import tpu as pltpu
from jax.sharding import PartitionSpec as P

HEAD_DIM = 64
epsilon = 1e-05
theta_base = 160000.0
masked_score = -1e30
BLOCK = 256
TAIL = 16
STAT_ROWS = 8
f32 = jnp.float32
bf16 = jnp.bfloat16


def dot_nn(left, right):
    return lax.dot_general(left, right, (((1,), (0,)), ((), ())), preferred_element_type=f32)


def dot_nt(left, right):
    return lax.dot_general(left, right, (((1,), (1,)), ((), ())), preferred_element_type=f32)


def dot_tn(left, right):
    return lax.dot_general(left, right, (((0,), (0,)), ((), ())), preferred_element_type=f32)


def block_rows(index):
    return pl.ds(pl.multiple_of(index * BLOCK, BLOCK), BLOCK)


def feature_block(index, distance, width):
    return pl.ds(pl.multiple_of((index ^ distance) * width, width), width)


def norm_parts(parts, full):
    mean = sum(jnp.sum(part, axis=-1, keepdims=True) for part in parts) / full
    parts = [part - mean for part in parts]
    spread = sum(jnp.sum(part * part, axis=-1, keepdims=True) for part in parts) / full
    factor = lax.rsqrt(spread + epsilon)
    return [part * factor for part in parts], mean, factor


def columns_to_rows(columns):
    lane = lax.broadcasted_iota(jnp.int32, (BLOCK, 128), 1)
    packed = jnp.zeros((BLOCK, 128), f32)
    for place, column in enumerate(columns):
        packed = jnp.where(lane == place, column, packed)
    return packed.T[0:STAT_ROWS, :]


def turn(values, cos_ref, low_ref, high_ref, rows, sign):
    parts = []
    for start in range(0, values.shape[1], 128):
        part = values[:, start : start + 128]
        swapped = pltpu.roll(part, 96, 1) * low_ref[rows, :] + pltpu.roll(part, 32, 1) * high_ref[
            rows, :
        ]
        parts.append(part * cos_ref[rows, :] + sign * swapped)
    return jnp.concatenate(parts, axis=1)


def head_only(values, head):
    lane = lax.broadcasted_iota(jnp.int32, values.shape, 1)
    inside = (lane >= head * HEAD_DIM) & (lane < (head + 1) * HEAD_DIM)
    return jnp.where(inside, values.astype(f32), 0.0).astype(bf16)


def send_tail(send, slots, first, second):
    lanes = send.shape[1]
    pieces = [row[:, start : start + lanes] for row in (first, second) for start in range(0, slots, lanes)]
    pieces.append(jnp.zeros((TAIL - len(pieces), lanes), f32))
    send[slots : slots + TAIL, :] = jnp.concatenate(pieces, axis=0).astype(bf16)


def attend_kernel(meta, *refs, count, width, heads, slots, full):
    pieces = refs[:count]
    gain, weight, cos_ref, low_ref, high_ref = refs[count : count + 5]
    normed, q_out, k_out, v_out, attended, log_sum, stats, keep, send = refs[count + 5 : count + 14]
    values_t, out_t = refs[count + 14 :]
    index = meta[0]
    length = meta[1]
    live = pl.cdiv(length, BLOCK)
    blocks = slots // BLOCK

    def project(block, carry):
        rows = block_rows(block)
        units, mean, factor = norm_parts([piece[rows, :].astype(f32) for piece in pieces], full)
        for place, unit in enumerate(units):
            gained = unit * gain[pl.ds(index ^ place, 1), :]
            normed[rows, feature_block(index, place, width)] = gained.astype(bf16)
        stats[:, rows] = columns_to_rows((mean, factor))
        row = normed[rows, :]
        turned = turn(dot_nn(row, weight[0]), cos_ref, low_ref, high_ref, rows, 1.0)
        q_out[rows, :] = (turned.astype(bf16).astype(f32) * HEAD_DIM**-0.5).astype(bf16)
        turned = turn(dot_nn(row, weight[1]), cos_ref, low_ref, high_ref, rows, 1.0)
        k_out[rows, :] = turned.astype(bf16)
        v_out[rows, :] = dot_nn(row, weight[2]).astype(bf16)
        return carry

    def clear(block, carry):
        rows = block_rows(block)
        normed[rows, :] = jnp.zeros((BLOCK, full), bf16)
        for ref in (q_out, k_out, v_out, attended):
            ref[rows, :] = jnp.zeros((BLOCK, width), bf16)
        stats[:, rows] = jnp.zeros((STAT_ROWS, BLOCK), f32)
        keep[rows, :] = jnp.zeros((BLOCK, keep.shape[1]), f32)
        send[rows, :] = jnp.zeros((BLOCK, send.shape[1]), bf16)
        return carry

    lax.fori_loop(0, live, project, 0)
    lax.fori_loop(live, blocks, clear, 0)
    log_sum[...] = jnp.zeros(log_sum.shape, f32)

    def attend(count_live):
        span = count_live * BLOCK
        values_t[:, 0:span] = v_out[0:span, :].T

        def query_block(block, carry):
            rows = block_rows(block)
            queries = q_out[rows, :]
            for head in range(heads):
                mine = slice(head * HEAD_DIM, (head + 1) * HEAD_DIM)
                scores = dot_nt(k_out[0:span, :], head_only(queries, head))
                slot = lax.broadcasted_iota(jnp.int32, (span, BLOCK), 0)
                scores = jnp.where(slot < length, scores, masked_score)
                top = jnp.max(scores, axis=0, keepdims=True)
                weights = jnp.exp(scores - top)
                total = jnp.sum(weights, axis=0, keepdims=True)
                result = dot_nn(values_t[mine, 0:span], weights.astype(bf16))
                out_t[mine, :] = result * (1.0 / total)
                log_sum[head : head + 1, rows] = top + jnp.log(total)
            attended[rows, :] = out_t[...].T.astype(bf16)
            return carry

        lax.fori_loop(0, count_live, query_block, 0)

    for count_live in range(1, blocks + 1):
        pl.when(live == count_live)(functools.partial(attend, count_live))

    def output(block, carry):
        rows = block_rows(block)
        row = attended[rows, :]
        for place in range(count):
            part = dot_nt(row, weight[3, feature_block(index, place, width), :])
            target = slice((place // 2) * width, (place // 2 + 1) * width)
            if place % 2:
                send[rows, target] = part.astype(bf16)
            else:
                keep[rows, target] = part
        return carry

    lax.fori_loop(0, live, output, 0)


def mlp_kernel(meta, *refs, count, width, slots, full):
    rows_in = refs[:count]
    grads_in = refs[count : 2 * count]
    gain, weight = refs[2 * count : 2 * count + 2]
    (normed, grads, mixed, grad_expanded, stats, out_keep, out_send, back_keep, back_send) = refs[
        2 * count + 2 :
    ]
    index = meta[0]
    length = meta[1]
    live = pl.cdiv(length, BLOCK)
    blocks = slots // BLOCK

    def step(block, carry):
        rows = block_rows(block)
        slot = block * BLOCK + lax.broadcasted_iota(jnp.int32, (BLOCK, 1), 0)
        units, mean, factor = norm_parts([piece[rows, :].astype(f32) for piece in rows_in], full)
        for place, unit in enumerate(units):
            here = feature_block(index, place, width)
            gained = unit * gain[pl.ds(index ^ place, 1), :]
            normed[rows, here] = gained.astype(bf16)
            grad = jnp.where(slot < length, grads_in[place][rows, :].astype(f32), 0.0)
            grads[rows, here] = grad.astype(bf16)
        row = normed[rows, :]
        grad = grads[rows, :]
        gate = dot_nn(row, weight[0])
        linear = dot_nn(row, weight[1])
        grad_mixed = dot_nn(grad, weight[2])
        phi = 0.5 + 0.5 * lax.erf(gate * (0.5**0.5))
        activated = gate * phi
        density = jnp.exp(-0.5 * gate * gate) * (0.5 / jnp.pi) ** 0.5
        mixed_low = (activated * linear).astype(bf16)
        mixed[rows, :] = mixed_low
        first = (grad_mixed * linear * (phi + gate * density)).astype(bf16)
        second = (grad_mixed * activated).astype(bf16)
        grad_expanded[0, rows, :] = first
        grad_expanded[1, rows, :] = second
        plain_sum = jnp.zeros((BLOCK, 1), f32)
        unit_sum = jnp.zeros((BLOCK, 1), f32)
        for place in range(count):
            here = feature_block(index, place, width)
            target = slice((place // 2) * width, (place // 2 + 1) * width)
            part = dot_nt(mixed_low, weight[2, here, :])
            back = dot_nt(first, weight[0, here, :]) + dot_nt(second, weight[1, here, :])
            plain_sum += jnp.sum(back * gain[pl.ds(index ^ place, 1), :], axis=-1, keepdims=True)
            unit_sum += jnp.sum(back * normed[rows, here].astype(f32), axis=-1, keepdims=True)
            if place % 2:
                out_send[rows, target] = part.astype(bf16)
                back_send[rows, target] = back.astype(bf16)
            else:
                out_keep[rows, target] = part
                back_keep[rows, target] = back
        stats[:, rows] = columns_to_rows((mean, factor, plain_sum, unit_sum))
        return carry

    def clear(block, carry):
        rows = block_rows(block)
        for ref in (normed, grads, mixed, out_keep, out_send, back_keep, back_send):
            ref[rows, :] = jnp.zeros((BLOCK, ref.shape[1]), ref.dtype)
        for place in range(2):
            grad_expanded[place, rows, :] = jnp.zeros((BLOCK, mixed.shape[1]), bf16)
        stats[:, rows] = jnp.zeros((STAT_ROWS, BLOCK), f32)
        return carry

    lax.fori_loop(0, live, step, 0)
    lax.fori_loop(live, blocks, clear, 0)
    send_tail(back_send, slots, stats[2:3, :], stats[3:4, :])


def attend_back_kernel(meta, *refs, count, width, heads, slots, full):
    grads_in = refs[:count]
    (q_in, k_in, v_in, attended, log_sum, normed, gain, weight, cos_ref, low_ref, high_ref) = refs[
        count : count + 11
    ]
    grads, grad_projected, stats, keep, send = refs[count + 11 : count + 16]
    (grad_att, delta, keys_t, probs_all, scores_all, query_t, key_total, value_total) = refs[
        count + 16 :
    ]
    index = meta[0]
    length = meta[1]
    live = pl.cdiv(length, BLOCK)
    blocks = slots // BLOCK

    def enter(block, carry):
        rows = block_rows(block)
        for place in range(count):
            grads[rows, feature_block(index, place, width)] = grads_in[place][rows, :]
        grad = dot_nn(grads[rows, :], weight[3]).astype(bf16)
        grad_att[rows, :] = grad
        inner = (grad.astype(f32) * attended[rows, :].astype(f32)).T
        for head in range(heads):
            mine = slice(head * HEAD_DIM, (head + 1) * HEAD_DIM)
            delta[head : head + 1, rows] = jnp.sum(inner[mine, :], axis=0, keepdims=True)
        return carry

    def clear(block, carry):
        rows = block_rows(block)
        grads[rows, :] = jnp.zeros((BLOCK, full), bf16)
        for place in range(3):
            grad_projected[place, rows, :] = jnp.zeros((BLOCK, width), bf16)
        stats[:, rows] = jnp.zeros((STAT_ROWS, BLOCK), f32)
        keep[rows, :] = jnp.zeros((BLOCK, keep.shape[1]), f32)
        send[rows, :] = jnp.zeros((BLOCK, send.shape[1]), bf16)
        return carry

    lax.fori_loop(0, live, enter, 0)
    lax.fori_loop(live, blocks, clear, 0)

    def attend(count_live):
        span = count_live * BLOCK
        keys_t[:, 0:span] = k_in[0:span, :].T
        key_total[0:span, :] = jnp.zeros((span, width), f32)
        value_total[0:span, :] = jnp.zeros((span, width), f32)

        def query_block(block, carry):
            rows = block_rows(block)
            queries = [head_only(q_in[rows, :], head) for head in range(heads)]
            grad_rows = [head_only(grad_att[rows, :], head) for head in range(heads)]
            for head in range(heads):
                mine = slice(head * HEAD_DIM, (head + 1) * HEAD_DIM)
                lanes = slice(head * BLOCK, (head + 1) * BLOCK)
                scores = dot_nt(k_in[0:span, :], queries[head])
                slot = lax.broadcasted_iota(jnp.int32, (span, BLOCK), 0)
                scores = jnp.where(slot < length, scores, masked_score)
                weights = jnp.exp(scores - log_sum[head : head + 1, rows])
                grad_weights = dot_nt(v_in[0:span, :], grad_rows[head])
                grad_scores = (weights * (grad_weights - delta[head : head + 1, rows])).astype(bf16)
                probs_all[0:span, lanes] = weights.astype(bf16)
                scores_all[0:span, lanes] = grad_scores
                query_t[mine, :] = dot_nn(keys_t[mine, 0:span], grad_scores)
            value_total[0:span, :] += dot_nn(probs_all[0:span, :], jnp.concatenate(grad_rows, axis=0))
            key_total[0:span, :] += dot_nn(scores_all[0:span, :], jnp.concatenate(queries, axis=0))
            turned = turn(query_t[...].T * HEAD_DIM**-0.5, cos_ref, low_ref, high_ref, rows, -1.0)
            grad_projected[0, rows, :] = turned.astype(bf16)
            return carry

        lax.fori_loop(0, count_live, query_block, 0)

    for count_live in range(1, blocks + 1):
        pl.when(live == count_live)(functools.partial(attend, count_live))

    def leave(block, carry):
        rows = block_rows(block)
        turned = turn(key_total[rows, :], cos_ref, low_ref, high_ref, rows, -1.0)
        grad_projected[1, rows, :] = turned.astype(bf16)
        grad_projected[2, rows, :] = value_total[rows, :].astype(bf16)
        plain_sum = jnp.zeros((BLOCK, 1), f32)
        unit_sum = jnp.zeros((BLOCK, 1), f32)
        for place in range(count):
            here = feature_block(index, place, width)
            target = slice((place // 2) * width, (place // 2 + 1) * width)
            back = sum(
                dot_nt(grad_projected[kind, rows, :], weight[kind, here, :]) for kind in range(3)
            )
            plain_sum += jnp.sum(back * gain[pl.ds(index ^ place, 1), :], axis=-1, keepdims=True)
            unit_sum += jnp.sum(back * normed[rows, here].astype(f32), axis=-1, keepdims=True)
            if place % 2:
                send[rows, target] = back.astype(bf16)
            else:
                keep[rows, target] = back
        zero = jnp.zeros((BLOCK, 1), f32)
        stats[:, rows] = columns_to_rows((zero, zero, plain_sum, unit_sum))
        return carry

    lax.fori_loop(0, live, leave, 0)
    send_tail(send, slots, stats[2:3, :], stats[3:4, :])


def grad_kernel(*refs, pairs, seq_count):
    out = refs[-1]
    place = 0
    cursor = 0
    for kinds in pairs:
        lefts = refs[cursor : cursor + seq_count]
        rights = refs[cursor + seq_count : cursor + 2 * seq_count]
        cursor += 2 * seq_count
        for kind in range(kinds):
            total = sum(dot_tn(left[...], right[kind]) for left, right in zip(lefts, rights))
            for step in range(out.shape[0]):
                rows = out.shape[2]
                out[step, place] = total[step * rows : (step + 1) * rows, :].astype(bf16)
            place += 1


def weight_grads(groups, wide_count, full):
    rows = full // wide_count
    per_step = max(BLOCK // rows, 1)
    columns = groups[0][1][0].shape[2]
    slots = groups[0][0][0].shape[0]
    seq_count = len(groups[0][0])
    pairs = tuple(rights[0].shape[0] for _, rights in groups)
    operands = []
    specs = []
    for lefts, rights in groups:
        for left in lefts:
            operands.append(left)
            specs.append(pl.BlockSpec((slots, rows * per_step), lambda step: (0, step)))
        for right in rights:
            operands.append(right)
            specs.append(pl.BlockSpec(right.shape, lambda step: (0, 0, 0)))
    kinds = sum(pairs)
    return pl.pallas_call(
        functools.partial(grad_kernel, pairs=pairs, seq_count=seq_count),
        grid=(wide_count // per_step,),
        in_specs=specs,
        out_specs=pl.BlockSpec((per_step, kinds, rows, columns), lambda step: (step, 0, 0, 0)),
        out_shape=jax.ShapeDtypeStruct((wide_count, kinds, rows, columns), bf16),
    )(*operands)


def whole(shape):
    return pl.BlockSpec(shape, lambda step, meta: (0,) * len(shape))


def call_kernel(body, meta, operands, specs, outs, scratch, name):
    return pl.pallas_call(
        body,
        grid_spec=pltpu.PrefetchScalarGridSpec(
            num_scalar_prefetch=1,
            grid=(1,),
            in_specs=specs,
            out_specs=[whole(shape) for shape, _ in outs],
            scratch_shapes=scratch,
        ),
        out_shape=[jax.ShapeDtypeStruct(shape, kind) for shape, kind in outs],
        name=name,
    )(meta, *operands)


def swap(values, distance, count):
    return lax.ppermute(values, "narrow", [(place, place ^ distance) for place in range(count)])


def gather_narrow(own, count):
    pieces = {0: own}
    distance = count // 2
    while distance:
        for place in sorted(pieces):
            pieces[place | distance] = swap(pieces[place], distance, count)
        distance //= 2
    return [pieces[place] for place in range(count)]


def reduce_narrow(keep, send, sums, count, width):
    slots = keep.shape[0]
    received = swap(send, 1, count)
    total = keep + received[:slots].astype(f32)
    if sums is not None:
        rows = 2 * slots // send.shape[1]
        sums = sums + received[slots : slots + rows].astype(f32).reshape(2, slots)
    distance = 2
    while distance < count:
        split = total.reshape(slots, -1, 2, width) if total.shape[1] > 2 * width else None
        if split is None:
            going, staying = total[:, width:], total[:, :width]
        else:
            going = split[:, :, 1].reshape(slots, -1)
            staying = split[:, :, 0].reshape(slots, -1)
        going = going.astype(bf16)
        if sums is not None:
            tail = sums.astype(bf16).reshape(-1, going.shape[1])
            rows = tail.shape[0]
            pad = -rows % TAIL
            going = jnp.concatenate([going, tail, jnp.zeros((pad, tail.shape[1]), bf16)], axis=0)
        received = swap(going, distance, count)
        total = staying + received[:slots].astype(f32)
        if sums is not None:
            sums = sums + received[slots : slots + rows].astype(f32).reshape(2, slots)
        distance *= 2
    return total, sums


def rotary_rows(slots):
    half = HEAD_DIM // 2
    inverse = theta_base ** (-2.0 * jnp.arange(half, dtype=f32) / HEAD_DIM)
    angles = jnp.arange(slots, dtype=f32)[:, None] * inverse[None, :]
    cos = jnp.cos(angles)
    sin = jnp.sin(angles)
    none = jnp.zeros_like(sin)
    copies = 128 // HEAD_DIM
    return (
        jnp.tile(jnp.concatenate([cos, cos], axis=1), (1, copies)),
        jnp.tile(jnp.concatenate([-sin, none], axis=1), (1, copies)),
        jnp.tile(jnp.concatenate([none, sin], axis=1), (1, copies)),
    )


def norm_back(gradient, rows, stats, sums, gain, full):
    unit = (rows - stats[0][:, None]) * stats[1][:, None]
    inner = gradient * gain - sums[0][:, None] / full - unit * (sums[1][:, None] / full)
    return stats[1][:, None] * inner, jnp.sum(gradient * unit, axis=0)


def shards(
    inputs,
    lengths,
    attn_gain,
    attn_in_weight,
    attn_out_weight,
    mlp_gain,
    mlp_in_weight,
    mlp_out_weight,
    cotangent,
):
    count = lax.axis_size("narrow")
    wide_count = lax.axis_size("wide")
    index = lax.axis_index("narrow").astype(jnp.int32)
    tokens, width = inputs.shape
    full = width * count
    seq_count = lengths.shape[0]
    slots = tokens // seq_count
    heads = width // HEAD_DIM
    hidden = mlp_in_weight.shape[2]
    half = count // 2 * width
    tables = rotary_rows(slots)
    seqs = range(seq_count)
    metas = [jnp.stack([index, lengths[seq].astype(jnp.int32)]) for seq in seqs]
    own_rows = [slice(seq * slots, (seq + 1) * slots) for seq in seqs]
    valid = [(jnp.arange(slots) < lengths[seq]).astype(f32)[:, None] for seq in seqs]

    attn_weight = lax.all_gather(
        jnp.concatenate([attn_in_weight, attn_out_weight.T[None]]), "wide", axis=1, tiled=True
    )
    mlp_weight = lax.all_gather(
        jnp.concatenate([mlp_in_weight, mlp_out_weight.T[None]]), "wide", axis=1, tiled=True
    )
    input_pieces = gather_narrow(inputs, count)
    grad_pieces = gather_narrow(cotangent, count)
    attn_gain_rows = attn_gain.reshape(count, width)
    mlp_gain_rows = mlp_gain.reshape(count, width)
    gain_one = lax.dynamic_slice_in_dim(attn_gain, index * width, width)
    gain_two = lax.dynamic_slice_in_dim(mlp_gain, index * width, width)

    def seq_spec(seq):
        return pl.BlockSpec((slots, width), lambda step, meta: (seq, 0))

    row_spec = whole((slots, width))
    table_specs = [whole((slots, 128))] * 3
    gain_spec = whole((count, width))
    attn_spec = whole(attn_weight.shape)
    sizes = dict(count=count, width=width, slots=slots, full=full)

    forward = []
    for seq in seqs:
        forward.append(
            call_kernel(
                functools.partial(attend_kernel, heads=heads, **sizes),
                metas[seq],
                [*input_pieces, attn_gain_rows, attn_weight, *tables],
                [seq_spec(seq)] * count + [gain_spec, attn_spec] + table_specs,
                [((slots, full), bf16)]
                + [((slots, width), bf16)] * 4
                + [((max(heads, STAT_ROWS), slots), f32), ((STAT_ROWS, slots), f32)]
                + [((slots, half), f32), ((slots, half), bf16)],
                [pltpu.VMEM((width, slots), bf16), pltpu.VMEM((width, BLOCK), f32)],
                "attend_forward",
            )
        )
    residuals = []
    for seq in seqs:
        attn_part, _ = reduce_narrow(forward[seq][7], forward[seq][8], None, count, width)
        residuals.append(inputs[own_rows[seq]].astype(f32) + attn_part)
    residual_pieces = [gather_narrow(residuals[seq].astype(bf16), count) for seq in seqs]

    middle = []
    for seq in seqs:
        middle.append(
            call_kernel(
                functools.partial(mlp_kernel, **sizes),
                metas[seq],
                [*residual_pieces[seq], *grad_pieces, mlp_gain_rows, mlp_weight],
                [row_spec] * count + [seq_spec(seq)] * count + [gain_spec, whole(mlp_weight.shape)],
                [((slots, full), bf16), ((slots, full), bf16), ((slots, hidden), bf16)]
                + [((2, slots, hidden), bf16), ((STAT_ROWS, slots), f32)]
                + [((slots, half), f32), ((slots, half), bf16)]
                + [((slots, half), f32), ((slots + TAIL, half), bf16)],
                [],
                "mlp_both",
            )
        )
    mlp_grads = weight_grads(
        [
            ([middle[seq][0] for seq in seqs], [middle[seq][3] for seq in seqs]),
            ([middle[seq][1] for seq in seqs], [middle[seq][2][None] for seq in seqs]),
        ],
        wide_count,
        full,
    )
    mlp_shard = lax.psum_scatter(
        mlp_grads.reshape(-1, hidden), "wide", scatter_dimension=0, tiled=True
    ).reshape(mlp_grads.shape[1:])

    grad_residuals = []
    mlp_gain_local = 0.0
    for seq in seqs:
        stats = middle[seq][4]
        gradient, sums = reduce_narrow(
            middle[seq][7], middle[seq][8], stats[2:4], count, width
        )
        back, gain_part = norm_back(gradient, residuals[seq], stats, sums, gain_two, full)
        grad_residuals.append(cotangent[own_rows[seq]].astype(f32) * valid[seq] + back)
        mlp_gain_local = mlp_gain_local + gain_part
    attn_grad_pieces = [gather_narrow(grad_residuals[seq].astype(bf16), count) for seq in seqs]
    outputs = []
    for seq in seqs:
        mlp_part, _ = reduce_narrow(middle[seq][5], middle[seq][6], None, count, width)
        outputs.append((residuals[seq] + mlp_part) * valid[seq])

    backward = []
    for seq in seqs:
        normed, queries, keys, values, attended, log_sum = forward[seq][:6]
        backward.append(
            call_kernel(
                functools.partial(attend_back_kernel, heads=heads, **sizes),
                metas[seq],
                [*attn_grad_pieces[seq], queries, keys, values, attended, log_sum, normed]
                + [attn_gain_rows, attn_weight, *tables],
                [row_spec] * (count + 4)
                + [whole(log_sum.shape), whole((slots, full)), gain_spec, attn_spec]
                + table_specs,
                [((slots, full), bf16), ((3, slots, width), bf16), ((STAT_ROWS, slots), f32)]
                + [((slots, half), f32), ((slots + TAIL, half), bf16)],
                [
                    pltpu.VMEM((slots, width), bf16),
                    pltpu.VMEM((max(heads, STAT_ROWS), slots), f32),
                    pltpu.VMEM((width, slots), bf16),
                    pltpu.VMEM((slots, heads * BLOCK), bf16),
                    pltpu.VMEM((slots, heads * BLOCK), bf16),
                    pltpu.VMEM((width, BLOCK), f32),
                    pltpu.VMEM((slots, width), f32),
                    pltpu.VMEM((slots, width), f32),
                ],
                "attend_backward",
            )
        )
    attn_grads = weight_grads(
        [
            ([forward[seq][0] for seq in seqs], [backward[seq][1] for seq in seqs]),
            ([backward[seq][0] for seq in seqs], [forward[seq][4][None] for seq in seqs]),
        ],
        wide_count,
        full,
    )
    attn_shard = lax.psum_scatter(
        attn_grads.reshape(-1, width), "wide", scatter_dimension=0, tiled=True
    ).reshape(attn_grads.shape[1:])

    inputs_grads = []
    attn_gain_local = 0.0
    for seq in seqs:
        gradient, sums = reduce_narrow(
            backward[seq][3], backward[seq][4], backward[seq][2][2:4], count, width
        )
        rows = inputs[own_rows[seq]].astype(f32)
        back, gain_part = norm_back(gradient, rows, forward[seq][6], sums, gain_one, full)
        inputs_grads.append(grad_residuals[seq] + back)
        attn_gain_local = attn_gain_local + gain_part
    gain_grads = lax.psum(jnp.stack([attn_gain_local, mlp_gain_local]), "wide")
    return (
        jnp.concatenate(outputs),
        jnp.concatenate(inputs_grads),
        gain_grads[0],
        attn_shard[:3].astype(f32),
        attn_shard[3].T.astype(f32),
        gain_grads[1],
        mlp_shard[:2].astype(f32),
        mlp_shard[2].T.astype(f32),
    )


def solution(mesh):
    in_specs = (
        P("wide", "narrow"),
        P("wide"),
        P(),
        P(None, "wide", "narrow"),
        P("narrow", "wide"),
        P(),
        P(None, "wide", "narrow"),
        P("narrow", "wide"),
        P("wide", "narrow"),
    )
    out_specs = (
        P("wide", "narrow"),
        P("wide", "narrow"),
        P("narrow"),
        P(None, "wide", "narrow"),
        P("narrow", "wide"),
        P("narrow"),
        P(None, "wide", "narrow"),
        P("narrow", "wide"),
    )
    return jax.shard_map(shards, mesh=mesh, in_specs=in_specs, out_specs=out_specs, check_vma=False)
```

```python
import functools

import jax
import jax.numpy as jnp
from jax import lax
from jax.experimental import pallas as pl
from jax.experimental.pallas import tpu as pltpu
from jax.sharding import PartitionSpec as P


HEAD_DIM = 64
epsilon = 1e-05
theta_base = 160000.0
masked_score = -1e30
BLOCK = 256
TAIL = 16
STAT_ROWS = 8
f32 = jnp.float32
bf16 = jnp.bfloat16


def dot_nn(left, right):
    return lax.dot_general(left, right, (((1,), (0,)), ((), ())), preferred_element_type=f32)


def dot_nt(left, right):
    return lax.dot_general(left, right, (((1,), (1,)), ((), ())), preferred_element_type=f32)


def dot_tn(left, right):
    return lax.dot_general(left, right, (((0,), (0,)), ((), ())), preferred_element_type=f32)


def block_rows(index):
    return pl.ds(pl.multiple_of(index * BLOCK, BLOCK), BLOCK)


def feature_block(index, distance, width):
    return pl.ds(pl.multiple_of((index ^ distance) * width, width), width)


def norm_parts(parts, full):
    mean = sum(jnp.sum(part, axis=-1, keepdims=True) for part in parts) / full
    parts = [part - mean for part in parts]
    spread = sum(jnp.sum(part * part, axis=-1, keepdims=True) for part in parts) / full
    factor = lax.rsqrt(spread + epsilon)
    return [part * factor for part in parts], mean, factor


def columns_to_rows(columns):
    lane = lax.broadcasted_iota(jnp.int32, (BLOCK, 128), 1)
    packed = jnp.zeros((BLOCK, 128), f32)
    for place, column in enumerate(columns):
        packed = jnp.where(lane == place, column, packed)
    return packed.T[0:STAT_ROWS, :]


def turn(values, cos_ref, low_ref, high_ref, rows, sign):
    parts = []
    for start in range(0, values.shape[1], 128):
        part = values[:, start : start + 128]
        swapped = pltpu.roll(part, 96, 1) * low_ref[rows, :] + pltpu.roll(part, 32, 1) * high_ref[
            rows, :
        ]
        parts.append(part * cos_ref[rows, :] + sign * swapped)
    return jnp.concatenate(parts, axis=1)


def head_only(values, head):
    lane = lax.broadcasted_iota(jnp.int32, values.shape, 1)
    inside = (lane >= head * HEAD_DIM) & (lane < (head + 1) * HEAD_DIM)
    return jnp.where(inside, values.astype(f32), 0.0).astype(bf16)


def send_tail(send, slots, first, second):
    lanes = send.shape[1]
    pieces = [row[:, start : start + lanes] for row in (first, second) for start in range(0, slots, lanes)]
    if len(pieces) < TAIL:
        pieces.append(jnp.zeros((TAIL - len(pieces), lanes), f32))
    send[slots : slots + TAIL, :] = jnp.concatenate(pieces, axis=0).astype(bf16)


def attend_kernel(place_ref, lengths, *refs, seq, count, width, heads, slots, full):
    pieces = refs[:count]
    gain, weight, cos_ref, low_ref, high_ref = refs[count : count + 5]
    normed, q_out, k_out, v_out, attended, log_sum, stats, keep, send = refs[count + 5 : count + 14]
    values_t, out_t = refs[count + 14 :]
    index = place_ref[0]
    length = lengths[seq]
    live = pl.cdiv(length, BLOCK)
    blocks = slots // BLOCK

    def project(block, carry):
        rows = block_rows(block)
        units, mean, factor = norm_parts([piece[rows, :].astype(f32) for piece in pieces], full)
        for place, unit in enumerate(units):
            gained = unit * gain[pl.ds(index ^ place, 1), :]
            normed[rows, feature_block(index, place, width)] = gained.astype(bf16)
        stats[:, rows] = columns_to_rows((mean, factor))
        row = normed[rows, :]
        turned = turn(dot_nn(row, weight[0]), cos_ref, low_ref, high_ref, rows, 1.0)
        q_out[rows, :] = (turned.astype(bf16).astype(f32) * HEAD_DIM**-0.5).astype(bf16)
        turned = turn(dot_nn(row, weight[1]), cos_ref, low_ref, high_ref, rows, 1.0)
        k_out[rows, :] = turned.astype(bf16)
        v_out[rows, :] = dot_nn(row, weight[2]).astype(bf16)
        return carry

    def clear(block, carry):
        rows = block_rows(block)
        normed[rows, :] = jnp.zeros((BLOCK, full), bf16)
        for ref in (q_out, k_out, v_out, attended):
            ref[rows, :] = jnp.zeros((BLOCK, width), bf16)
        stats[:, rows] = jnp.zeros((STAT_ROWS, BLOCK), f32)
        keep[rows, :] = jnp.zeros((BLOCK, keep.shape[1]), f32)
        send[rows, :] = jnp.zeros((BLOCK, send.shape[1]), bf16)
        return carry

    lax.fori_loop(0, live, project, 0)
    lax.fori_loop(live, blocks, clear, 0)
    log_sum[...] = jnp.zeros(log_sum.shape, f32)

    def attend(count_live):
        span = count_live * BLOCK
        values_t[:, 0:span] = v_out[0:span, :].T

        def query_block(block, carry):
            rows = block_rows(block)
            queries = q_out[rows, :]
            for head in range(heads):
                mine = slice(head * HEAD_DIM, (head + 1) * HEAD_DIM)
                scores = dot_nt(k_out[0:span, :], head_only(queries, head))
                slot = lax.broadcasted_iota(jnp.int32, (span, BLOCK), 0)
                scores = jnp.where(slot < length, scores, masked_score)
                top = jnp.max(scores, axis=0, keepdims=True)
                weights = jnp.exp(scores - top)
                total = jnp.sum(weights, axis=0, keepdims=True)
                result = dot_nn(values_t[mine, 0:span], weights.astype(bf16))
                out_t[mine, :] = result * (1.0 / total)
                log_sum[head : head + 1, rows] = top + jnp.log(total)
            attended[rows, :] = out_t[...].T.astype(bf16)
            return carry

        lax.fori_loop(0, count_live, query_block, 0)

    for count_live in range(1, blocks + 1):
        pl.when(live == count_live)(functools.partial(attend, count_live))

    def output(block, carry):
        rows = block_rows(block)
        row = attended[rows, :]
        for place in range(count):
            part = dot_nt(row, weight[3, feature_block(index, place, width), :])
            target = slice((place // 2) * width, (place // 2 + 1) * width)
            if place % 2:
                send[rows, target] = part.astype(bf16)
            else:
                keep[rows, target] = part
        return carry

    lax.fori_loop(0, live, output, 0)


def mlp_kernel(place_ref, lengths, *refs, seq, count, width, slots, full):
    rows_in = refs[:count]
    grads_in = refs[count : 2 * count]
    gain, weight = refs[2 * count : 2 * count + 2]
    (normed, grads, mixed, grad_expanded, stats, out_keep, out_send, back_keep, back_send) = refs[
        2 * count + 2 :
    ]
    index = place_ref[0]
    length = lengths[seq]
    live = pl.cdiv(length, BLOCK)
    blocks = slots // BLOCK

    def step(block, carry):
        rows = block_rows(block)
        slot = block * BLOCK + lax.broadcasted_iota(jnp.int32, (BLOCK, 1), 0)
        units, mean, factor = norm_parts([piece[rows, :].astype(f32) for piece in rows_in], full)
        for place, unit in enumerate(units):
            here = feature_block(index, place, width)
            gained = unit * gain[pl.ds(index ^ place, 1), :]
            normed[rows, here] = gained.astype(bf16)
            grad = jnp.where(slot < length, grads_in[place][rows, :].astype(f32), 0.0)
            grads[rows, here] = grad.astype(bf16)
        row = normed[rows, :]
        grad = grads[rows, :]
        gate = dot_nn(row, weight[0])
        linear = dot_nn(row, weight[1])
        grad_mixed = dot_nn(grad, weight[2])
        phi = 0.5 + 0.5 * lax.erf(gate * (0.5**0.5))
        activated = gate * phi
        density = jnp.exp(-0.5 * gate * gate) * (0.5 / jnp.pi) ** 0.5
        mixed_low = (activated * linear).astype(bf16)
        mixed[rows, :] = mixed_low
        first = (grad_mixed * linear * (phi + gate * density)).astype(bf16)
        second = (grad_mixed * activated).astype(bf16)
        grad_expanded[0, rows, :] = first
        grad_expanded[1, rows, :] = second
        plain_sum = jnp.zeros((BLOCK, 1), f32)
        unit_sum = jnp.zeros((BLOCK, 1), f32)
        for place in range(count):
            here = feature_block(index, place, width)
            target = slice((place // 2) * width, (place // 2 + 1) * width)
            part = dot_nt(mixed_low, weight[2, here, :])
            back = dot_nt(first, weight[0, here, :]) + dot_nt(second, weight[1, here, :])
            plain_sum += jnp.sum(back * gain[pl.ds(index ^ place, 1), :], axis=-1, keepdims=True)
            unit_sum += jnp.sum(back * normed[rows, here].astype(f32), axis=-1, keepdims=True)
            if place % 2:
                out_send[rows, target] = part.astype(bf16)
                back_send[rows, target] = back.astype(bf16)
            else:
                out_keep[rows, target] = part
                back_keep[rows, target] = back
        stats[:, rows] = columns_to_rows((mean, factor, plain_sum, unit_sum))
        return carry

    def clear(block, carry):
        rows = block_rows(block)
        for ref in (normed, grads, mixed, out_keep, out_send, back_keep, back_send):
            ref[rows, :] = jnp.zeros((BLOCK, ref.shape[1]), ref.dtype)
        for place in range(2):
            grad_expanded[place, rows, :] = jnp.zeros((BLOCK, mixed.shape[1]), bf16)
        stats[:, rows] = jnp.zeros((STAT_ROWS, BLOCK), f32)
        return carry

    lax.fori_loop(0, live, step, 0)
    lax.fori_loop(live, blocks, clear, 0)
    send_tail(back_send, slots, stats[2:3, :], stats[3:4, :])


def attend_back_kernel(place_ref, lengths, *refs, seq, count, width, heads, slots, full):
    grads_in = refs[:count]
    (q_in, k_in, v_in, attended, log_sum, normed, gain, weight, cos_ref, low_ref, high_ref) = refs[
        count : count + 11
    ]
    grads, grad_projected, stats, keep, send = refs[count + 11 : count + 16]
    (grad_att, delta, keys_t, probs_all, scores_all, query_t, key_total, value_total) = refs[
        count + 16 :
    ]
    index = place_ref[0]
    length = lengths[seq]
    live = pl.cdiv(length, BLOCK)
    blocks = slots // BLOCK

    def enter(block, carry):
        rows = block_rows(block)
        for place in range(count):
            grads[rows, feature_block(index, place, width)] = grads_in[place][rows, :]
        grad = dot_nn(grads[rows, :], weight[3]).astype(bf16)
        grad_att[rows, :] = grad
        inner = (grad.astype(f32) * attended[rows, :].astype(f32)).T
        for head in range(heads):
            mine = slice(head * HEAD_DIM, (head + 1) * HEAD_DIM)
            delta[head : head + 1, rows] = jnp.sum(inner[mine, :], axis=0, keepdims=True)
        return carry

    def clear(block, carry):
        rows = block_rows(block)
        grads[rows, :] = jnp.zeros((BLOCK, full), bf16)
        for place in range(3):
            grad_projected[place, rows, :] = jnp.zeros((BLOCK, width), bf16)
        stats[:, rows] = jnp.zeros((STAT_ROWS, BLOCK), f32)
        keep[rows, :] = jnp.zeros((BLOCK, keep.shape[1]), f32)
        send[rows, :] = jnp.zeros((BLOCK, send.shape[1]), bf16)
        return carry

    lax.fori_loop(0, live, enter, 0)
    lax.fori_loop(live, blocks, clear, 0)

    def attend(count_live):
        span = count_live * BLOCK
        keys_t[:, 0:span] = k_in[0:span, :].T
        key_total[0:span, :] = jnp.zeros((span, width), f32)
        value_total[0:span, :] = jnp.zeros((span, width), f32)

        def query_block(block, carry):
            rows = block_rows(block)
            queries = [head_only(q_in[rows, :], head) for head in range(heads)]
            grad_rows = [head_only(grad_att[rows, :], head) for head in range(heads)]
            for head in range(heads):
                mine = slice(head * HEAD_DIM, (head + 1) * HEAD_DIM)
                lanes = slice(head * BLOCK, (head + 1) * BLOCK)
                scores = dot_nt(k_in[0:span, :], queries[head])
                slot = lax.broadcasted_iota(jnp.int32, (span, BLOCK), 0)
                scores = jnp.where(slot < length, scores, masked_score)
                weights = jnp.exp(scores - log_sum[head : head + 1, rows])
                grad_weights = dot_nt(v_in[0:span, :], grad_rows[head])
                grad_scores = (weights * (grad_weights - delta[head : head + 1, rows])).astype(bf16)
                probs_all[0:span, lanes] = weights.astype(bf16)
                scores_all[0:span, lanes] = grad_scores
                query_t[mine, :] = dot_nn(keys_t[mine, 0:span], grad_scores)
            value_total[0:span, :] += dot_nn(probs_all[0:span, :], jnp.concatenate(grad_rows, axis=0))
            key_total[0:span, :] += dot_nn(scores_all[0:span, :], jnp.concatenate(queries, axis=0))
            turned = turn(query_t[...].T * HEAD_DIM**-0.5, cos_ref, low_ref, high_ref, rows, -1.0)
            grad_projected[0, rows, :] = turned.astype(bf16)
            return carry

        lax.fori_loop(0, count_live, query_block, 0)

    for count_live in range(1, blocks + 1):
        pl.when(live == count_live)(functools.partial(attend, count_live))

    def leave(block, carry):
        rows = block_rows(block)
        turned = turn(key_total[rows, :], cos_ref, low_ref, high_ref, rows, -1.0)
        grad_projected[1, rows, :] = turned.astype(bf16)
        grad_projected[2, rows, :] = value_total[rows, :].astype(bf16)
        plain_sum = jnp.zeros((BLOCK, 1), f32)
        unit_sum = jnp.zeros((BLOCK, 1), f32)
        for place in range(count):
            here = feature_block(index, place, width)
            target = slice((place // 2) * width, (place // 2 + 1) * width)
            back = sum(
                dot_nt(grad_projected[kind, rows, :], weight[kind, here, :]) for kind in range(3)
            )
            plain_sum += jnp.sum(back * gain[pl.ds(index ^ place, 1), :], axis=-1, keepdims=True)
            unit_sum += jnp.sum(back * normed[rows, here].astype(f32), axis=-1, keepdims=True)
            if place % 2:
                send[rows, target] = back.astype(bf16)
            else:
                keep[rows, target] = back
        zero = jnp.zeros((BLOCK, 1), f32)
        stats[:, rows] = columns_to_rows((zero, zero, plain_sum, unit_sum))
        return carry

    lax.fori_loop(0, live, leave, 0)
    send_tail(send, slots, stats[2:3, :], stats[3:4, :])


def rows_to_columns(rows):
    filler = jnp.zeros((128 - len(rows), BLOCK), f32)
    return jnp.concatenate([*rows, filler], axis=0).T


def read_tail(tail, slots):
    values = tail[...].astype(f32)
    lanes = values.shape[1]
    lines = slots // lanes
    return [
        jnp.concatenate([values[row : row + 1] for row in range(start, start + lines)], axis=1)
        for start in (0, lines)
    ]


def near_kernel(*refs, width, slots, tailed):
    if tailed:
        keep, received, tail, sums, going, staying, sums_out = refs
    else:
        keep, received, going, staying = refs
    step = pl.program_id(0)
    total = keep[...] + received[...].astype(f32)
    for block in range(total.shape[1] // width):
        part = total[:, block * width : (block + 1) * width]
        target = slice((block // 2) * width, (block // 2 + 1) * width)
        if block % 2:
            going[block_rows(step), target] = part.astype(bf16)
        else:
            staying[:, target] = part
    if tailed:

        @pl.when(step == 0)
        def _():
            plain, unit = read_tail(tail, slots)
            plain = plain + sums[2:3, :]
            unit = unit + sums[3:4, :]
            empty = jnp.zeros((2, slots), f32)
            sums_out[...] = jnp.concatenate([empty, plain, unit, empty, empty], axis=0)
            send_tail(going, slots, plain, unit)


def residual_kernel(inputs, staying, received, out, low):
    total = inputs[...].astype(f32) + staying[...] + received[...].astype(f32)
    out[...] = total
    low[...] = total.astype(bf16)


def output_kernel(place_ref, lengths, residual, staying, received, *rest, seq):
    out = rest[-1]
    slot = pl.program_id(0) * BLOCK + lax.broadcasted_iota(jnp.int32, (BLOCK, 1), 0)
    total = residual[...] + (staying[...] + received[...].astype(f32))
    out[...] = jnp.where(slot < lengths[seq], total, 0.0)


def norm_back_kernel(place_ref, lengths, *refs, seq, slots, full, masked):
    (staying, received, tail, sums, stats, source, base, gain) = refs[:8]
    low = refs[-2] if masked else None
    out = refs[-3] if masked else refs[-2]
    gain_grad = refs[-1]
    step = pl.program_id(0)
    plain, unit_sum = read_tail(tail, slots)
    here = block_rows(step)
    columns = rows_to_columns([stats[0:1, here], stats[1:2, here], sums[2:3, here], sums[3:4, here]])
    lane_block = [plain[:, start : start + BLOCK] for start in range(0, slots, BLOCK)]
    unit_block = [unit_sum[:, start : start + BLOCK] for start in range(0, slots, BLOCK)]
    more_plain = lane_block[0]
    more_unit = unit_block[0]
    for place in range(1, len(lane_block)):
        more_plain = jnp.where(step == place, lane_block[place], more_plain)
        more_unit = jnp.where(step == place, unit_block[place], more_unit)
    more = rows_to_columns([more_plain, more_unit])
    mean, factor = columns[:, 0:1], columns[:, 1:2]
    plain_mean = (columns[:, 2:3] + more[:, 0:1]) / full
    unit_mean = (columns[:, 3:4] + more[:, 1:2]) / full
    unit = (source[...].astype(f32) - mean) * factor
    gradient = staying[...] + received[...].astype(f32)
    inner = gradient * gain[pl.ds(place_ref[0], 1), :] - plain_mean - unit * unit_mean
    below = base[...].astype(f32)
    if masked:
        slot = step * BLOCK + lax.broadcasted_iota(jnp.int32, (BLOCK, 1), 0)
        below = jnp.where(slot < lengths[seq], below, 0.0)
    total = below + factor * inner
    out[...] = total
    if masked:
        low[...] = total.astype(bf16)

    @pl.when(step == 0)
    def _():
        gain_grad[...] = jnp.zeros(gain_grad.shape, f32)

    gain_grad[0:1, :] += jnp.sum(gradient * unit, axis=0, keepdims=True)


def grad_kernel(*refs, pairs, seq_count):
    out = refs[-1]
    place = 0
    cursor = 0
    for kinds in pairs:
        lefts = refs[cursor : cursor + seq_count]
        rights = refs[cursor + seq_count : cursor + 2 * seq_count]
        cursor += 2 * seq_count
        for kind in range(kinds):
            total = sum(dot_tn(left[...], right[kind]) for left, right in zip(lefts, rights))
            for step in range(out.shape[0]):
                rows = out.shape[2]
                out[step, place] = total[step * rows : (step + 1) * rows, :].astype(bf16)
            place += 1


def weight_grads(groups, wide_count, full, micros, earlier):
    rows = full // wide_count
    per_step = max(BLOCK // rows, 1)
    columns = groups[0][1][0].shape[2]
    slots = groups[0][0][0].shape[0]
    seq_count = len(groups[0][0])
    pairs = tuple(rights[0].shape[0] for _, rights in groups)
    operands = []
    specs = []
    for lefts, rights in groups:
        for left in lefts:
            operands.append(left)
            specs.append(pl.BlockSpec((slots, rows * per_step), lambda step: (0, step)))
        for right in rights:
            operands.append(right)
            specs.append(pl.BlockSpec(right.shape, lambda step: (0, 0, 0)))
    kinds = sum(pairs)
    body = functools.partial(grad_kernel, pairs=pairs, seq_count=seq_count)
    body, operands, specs = after(body, operands, specs, earlier, 0)
    return pl.pallas_call(
        body,
        grid=(wide_count // per_step,),
        in_specs=specs,
        out_specs=pl.BlockSpec((per_step, kinds, rows, columns), lambda step: (step, 0, 0, 0)),
        out_shape=jax.ShapeDtypeStruct((wide_count, kinds, rows, columns), bf16),
        cost_estimate=estimate(micros),
    )(*operands)


def whole(shape):
    return pl.BlockSpec(shape, lambda step, *scalars: (0,) * len(shape))


def striped(columns, seq=0, blocks=0):
    return pl.BlockSpec((BLOCK, columns), lambda step, *scalars: (seq * blocks + step, 0))


def tail_spec(columns, slots):
    return pl.BlockSpec((TAIL, columns), lambda step, *scalars: (slots // TAIL, 0))


def after(body, operands, specs, earlier, scalars):
    place = scalars + len(operands)

    def ordered(*refs):
        return body(*refs[:place], *refs[place + len(earlier) :])

    unread = [pl.BlockSpec(memory_space=pl.ANY)] * len(earlier)
    return ordered, [*operands, *earlier], [*specs, *unread]


def estimate(micros):
    return pl.CostEstimate(flops=int(micros * 1e9), transcendentals=0, bytes_accessed=1 << 20)


def glue_call(body, scalars, operands, specs, outs, out_specs, steps, aliases=()):
    return pl.pallas_call(
        body,
        grid_spec=pltpu.PrefetchScalarGridSpec(
            num_scalar_prefetch=len(scalars), grid=(steps,), in_specs=specs, out_specs=out_specs
        ),
        out_shape=[jax.ShapeDtypeStruct(shape, kind) for shape, kind in outs],
        input_output_aliases=dict(aliases),
        cost_estimate=estimate(2),
    )(*scalars, *operands)


def call_kernel(body, meta, operands, specs, outs, scratch, micros, earlier):
    body, operands, specs = after(body, operands, specs, earlier, 2)
    return pl.pallas_call(
        body,
        grid_spec=pltpu.PrefetchScalarGridSpec(
            num_scalar_prefetch=2,
            grid=(1,),
            in_specs=specs,
            out_specs=[whole(shape) for shape, _ in outs],
            scratch_shapes=scratch,
        ),
        out_shape=[jax.ShapeDtypeStruct(shape, kind) for shape, kind in outs],
        cost_estimate=estimate(micros),
    )(*meta, *operands)


def swap(values, distance, count):
    return lax.ppermute(values, "narrow", [(place, place ^ distance) for place in range(count)])


def gather_narrow(own, count):
    pieces = {0: own}
    distance = count // 2
    while distance:
        for place in sorted(pieces):
            pieces[place | distance] = swap(pieces[place], distance, count)
        distance //= 2
    return [pieces[place] for place in range(count)]


def reduce_narrow(keep, send, sums, count, width):
    slots = keep.shape[0]
    tailed = sums is not None
    received = swap(send, 1, count)
    distance = 2
    while distance < count:
        lanes = keep.shape[1]
        operands = [keep, received]
        specs = [striped(lanes), striped(lanes)]
        outs = [((slots + TAIL * tailed, lanes // 2), bf16), ((slots, lanes // 2), f32)]
        out_specs = [whole(outs[0][0]), striped(lanes // 2)]
        if tailed:
            operands += [received, sums]
            specs += [tail_spec(lanes, slots), whole(sums.shape)]
            outs.append((sums.shape, f32))
            out_specs.append(whole(sums.shape))
        body = functools.partial(near_kernel, width=width, slots=slots, tailed=tailed)
        going, keep, *rest = glue_call(body, (), operands, specs, outs, out_specs, slots // BLOCK)
        if tailed:
            sums = rest[0]
        received = swap(going, distance, count)
        distance *= 2
    return keep, received, sums


def rotary_rows(slots):
    half = HEAD_DIM // 2
    inverse = theta_base ** (-2.0 * jnp.arange(half, dtype=f32) / HEAD_DIM)
    angles = jnp.arange(slots, dtype=f32)[:, None] * inverse[None, :]
    cos = jnp.cos(angles)
    sin = jnp.sin(angles)
    none = jnp.zeros_like(sin)
    copies = 128 // HEAD_DIM
    return (
        jnp.tile(jnp.concatenate([cos, cos], axis=1), (1, copies)),
        jnp.tile(jnp.concatenate([-sin, none], axis=1), (1, copies)),
        jnp.tile(jnp.concatenate([none, sin], axis=1), (1, copies)),
    )


def shards(
    inputs,
    lengths,
    attn_gain,
    attn_in_weight,
    attn_out_weight,
    mlp_gain,
    mlp_in_weight,
    mlp_out_weight,
    cotangent,
):
    count = lax.axis_size("narrow")
    wide_count = lax.axis_size("wide")
    index = lax.axis_index("narrow").astype(jnp.int32)
    tokens, width = inputs.shape
    full = width * count
    seq_count = lengths.shape[0]
    slots = tokens // seq_count
    heads = width // HEAD_DIM
    hidden = mlp_in_weight.shape[2]
    half = count // 2 * width
    tables = rotary_rows(slots)
    seqs = range(seq_count)
    blocks = slots // BLOCK
    meta = (index.reshape(1), lengths)

    attn_weight = lax.all_gather(
        jnp.concatenate([attn_in_weight, attn_out_weight.T[None]]), "wide", axis=1, tiled=True
    )
    mlp_weight = lax.all_gather(
        jnp.concatenate([mlp_in_weight, mlp_out_weight.T[None]]), "wide", axis=1, tiled=True
    )
    input_pieces = gather_narrow(inputs, count)
    grad_pieces = gather_narrow(cotangent, count)
    attn_gain_rows = attn_gain.reshape(count, width)
    mlp_gain_rows = mlp_gain.reshape(count, width)

    def seq_spec(seq):
        return pl.BlockSpec((slots, width), lambda step, *scalars: (seq, 0))

    row_spec = whole((slots, width))
    table_specs = [whole((slots, 128))] * 3
    gain_spec = whole((count, width))
    attn_spec = whole(attn_weight.shape)
    sizes = dict(count=count, width=width, slots=slots, full=full)

    def forward_call(seq, earlier):
        return call_kernel(
            functools.partial(attend_kernel, seq=seq, heads=heads, **sizes),
            meta,
            [*input_pieces, attn_gain_rows, attn_weight, *tables],
            [seq_spec(seq)] * count + [gain_spec, attn_spec] + table_specs,
            [((slots, full), bf16)]
            + [((slots, width), bf16)] * 4
            + [((max(heads, STAT_ROWS), slots), f32), ((STAT_ROWS, slots), f32)]
            + [((slots, half), f32), ((slots, half), bf16)],
            [pltpu.VMEM((width, slots), bf16), pltpu.VMEM((width, BLOCK), f32)],
            24,
            earlier,
        )

    def middle_call(seq, earlier):
        return call_kernel(
            functools.partial(mlp_kernel, seq=seq, **sizes),
            meta,
            [*residual_pieces[seq], *grad_pieces, mlp_gain_rows, mlp_weight],
            [row_spec] * count + [seq_spec(seq)] * count + [gain_spec, whole(mlp_weight.shape)],
            [((slots, full), bf16), ((slots, full), bf16), ((slots, hidden), bf16)]
            + [((2, slots, hidden), bf16), ((STAT_ROWS, slots), f32)]
            + [((slots, half), f32), ((slots, half), bf16)]
            + [((slots, half), f32), ((slots + TAIL, half), bf16)],
            [],
            24,
            earlier,
        )

    def backward_call(seq, earlier):
        normed, queries, keys, values, attended, log_sum = forward[seq][:6]
        return call_kernel(
            functools.partial(attend_back_kernel, seq=seq, heads=heads, **sizes),
            meta,
            [*attn_grad_pieces[seq], queries, keys, values, attended, log_sum, normed]
            + [attn_gain_rows, attn_weight, *tables],
            [row_spec] * (count + 4)
            + [whole(log_sum.shape), whole((slots, full)), gain_spec, attn_spec]
            + table_specs,
            [((slots, full), bf16), ((3, slots, width), bf16), ((STAT_ROWS, slots), f32)]
            + [((slots, half), f32), ((slots + TAIL, half), bf16)],
            [
                pltpu.VMEM((slots, width), bf16),
                pltpu.VMEM((max(heads, STAT_ROWS), slots), f32),
                pltpu.VMEM((width, slots), bf16),
                pltpu.VMEM((slots, heads * BLOCK), bf16),
                pltpu.VMEM((slots, heads * BLOCK), bf16),
                pltpu.VMEM((width, BLOCK), f32),
                pltpu.VMEM((slots, width), f32),
                pltpu.VMEM((slots, width), f32),
            ],
            26,
            earlier,
        )

    def norm_back_call(seq, parts, source, base, gains, target=None):
        staying, received, sums, stats = parts
        masked = target is None
        target = target or []
        outs = [((slots, width), f32), ((slots, width), bf16)]
        out_specs = [striped(width)] * 2
        if not masked:
            outs = [((tokens, width), f32)]
            out_specs = [striped(width, seq, blocks)]
        return glue_call(
            functools.partial(norm_back_kernel, seq=seq, slots=slots, full=full, masked=masked),
            meta,
            [staying, received, received, sums, stats, source[0], base[0], gains, *target],
            [striped(width), striped(width), tail_spec(width, slots)]
            + [whole(sums.shape), whole(stats.shape), source[1], base[1], gain_spec]
            + [pl.BlockSpec(memory_space=pl.ANY)] * len(target),
            [*outs, ((STAT_ROWS, width), f32)],
            [*out_specs, whole((STAT_ROWS, width))],
            blocks,
            [(10, 0)] * len(target),
        )

    forward, residuals, residual_pieces = [], [], []
    earlier = [grad_pieces[count // 2]]
    for seq in seqs:
        forward.append(forward_call(seq, earlier))
        earlier = [forward[seq][6]]
    for seq in seqs:
        staying, received, _ = reduce_narrow(forward[seq][7], forward[seq][8], None, count, width)
        residual, low = glue_call(
            residual_kernel,
            (),
            [inputs, staying, received],
            [striped(width, seq, blocks), striped(width), striped(width)],
            [((slots, width), f32), ((slots, width), bf16)],
            [striped(width)] * 2,
            blocks,
        )
        residuals.append(residual)
        residual_pieces.append(gather_narrow(low, count))

    middle, grad_residuals, attn_grad_pieces = [], [], []
    mlp_gain_local = 0.0
    for seq in seqs:
        middle.append(middle_call(seq, earlier))
        earlier = [middle[seq][4]]
    for seq in seqs:
        staying, received, sums = reduce_narrow(
            middle[seq][7], middle[seq][8], middle[seq][4], count, width
        )
        grad_residual, low, gain_part = norm_back_call(
            seq,
            (staying, received, sums, middle[seq][4]),
            (residuals[seq], striped(width)),
            (cotangent, striped(width, seq, blocks)),
            mlp_gain_rows,
        )
        grad_residuals.append(grad_residual)
        mlp_gain_local = mlp_gain_local + gain_part[0]
        attn_grad_pieces.append(gather_narrow(low, count))
    mlp_grads = weight_grads(
        [
            ([middle[seq][0] for seq in seqs], [middle[seq][3] for seq in seqs]),
            ([middle[seq][1] for seq in seqs], [middle[seq][2][None] for seq in seqs]),
        ],
        wide_count,
        full,
        17,
        earlier,
    )
    mlp_shard = lax.psum_scatter(
        mlp_grads.reshape(-1, hidden), "wide", scatter_dimension=0, tiled=True
    )

    backward, output, inputs_grad = [], [], []
    earlier = [mlp_grads]
    for seq in seqs:
        backward.append(backward_call(seq, earlier))
        earlier = [backward[seq][2]]
    for seq in seqs:
        staying, received, _ = reduce_narrow(middle[seq][5], middle[seq][6], None, count, width)
        output = glue_call(
            functools.partial(output_kernel, seq=seq),
            meta,
            [residuals[seq], staying, received, *output],
            [striped(width)] * 3 + [pl.BlockSpec(memory_space=pl.ANY)] * len(output),
            [((tokens, width), f32)],
            [striped(width, seq, blocks)],
            blocks,
            [(5, 0)] * len(output),
        )
    attn_grads = weight_grads(
        [
            ([forward[seq][0] for seq in seqs], [backward[seq][1] for seq in seqs]),
            ([backward[seq][0] for seq in seqs], [forward[seq][4][None] for seq in seqs]),
        ],
        wide_count,
        full,
        10,
        [*earlier, mlp_shard],
    )
    mlp_shard = mlp_shard.reshape(mlp_grads.shape[1:])
    attn_shard = lax.psum_scatter(
        attn_grads.reshape(-1, width), "wide", scatter_dimension=0, tiled=True
    ).reshape(attn_grads.shape[1:])

    attn_gain_local = 0.0
    for seq in seqs:
        staying, received, sums = reduce_narrow(
            backward[seq][3], backward[seq][4], backward[seq][2], count, width
        )
        *inputs_grad, gain_part = norm_back_call(
            seq,
            (staying, received, sums, forward[seq][6]),
            (inputs, striped(width, seq, blocks)),
            (grad_residuals[seq], striped(width)),
            attn_gain_rows,
            inputs_grad,
        )
        attn_gain_local = attn_gain_local + gain_part[0]
    gain_grads = lax.psum(jnp.stack([attn_gain_local, mlp_gain_local]), "wide")
    return (
        output[0],
        inputs_grad[0],
        gain_grads[0],
        attn_shard[:3].astype(f32),
        attn_shard[3].T.astype(f32),
        gain_grads[1],
        mlp_shard[:2].astype(f32),
        mlp_shard[2].T.astype(f32),
    )


def solution(mesh):
    in_specs = (
        P("wide", "narrow"),
        P("wide"),
        P(),
        P(None, "wide", "narrow"),
        P("narrow", "wide"),
        P(),
        P(None, "wide", "narrow"),
        P("narrow", "wide"),
        P("wide", "narrow"),
    )
    out_specs = (
        P("wide", "narrow"),
        P("wide", "narrow"),
        P("narrow"),
        P(None, "wide", "narrow"),
        P("narrow", "wide"),
        P("narrow"),
        P(None, "wide", "narrow"),
        P("narrow", "wide"),
    )
    return jax.shard_map(shards, mesh=mesh, in_specs=in_specs, out_specs=out_specs, check_vma=False)
```

```python
import functools

import jax
import jax.numpy as jnp
from jax import lax
from jax.experimental import pallas as pl
from jax.experimental.pallas import tpu as pltpu
from jax.sharding import PartitionSpec as P


HEAD_DIM = 64
epsilon = 1e-05
theta_base = 160000.0
masked_score = -1e30
BLOCK = 256
GLUE = 512
TAIL = 16
STAT_ROWS = 8
f32 = jnp.float32
bf16 = jnp.bfloat16


def dot_nn(left, right):
    return lax.dot_general(left, right, (((1,), (0,)), ((), ())), preferred_element_type=f32)


def dot_nt(left, right):
    return lax.dot_general(left, right, (((1,), (1,)), ((), ())), preferred_element_type=f32)


def dot_tn(left, right):
    return lax.dot_general(left, right, (((0,), (0,)), ((), ())), preferred_element_type=f32)


def block_rows(index):
    return pl.ds(pl.multiple_of(index * BLOCK, BLOCK), BLOCK)


def feature_block(index, distance, width):
    return pl.ds(pl.multiple_of((index ^ distance) * width, width), width)


def norm_parts(parts, full):
    mean = sum(jnp.sum(part, axis=-1, keepdims=True) for part in parts) / full
    parts = [part - mean for part in parts]
    spread = sum(jnp.sum(part * part, axis=-1, keepdims=True) for part in parts) / full
    factor = lax.rsqrt(spread + epsilon)
    return [part * factor for part in parts], mean, factor


def columns_to_rows(columns):
    lane = lax.broadcasted_iota(jnp.int32, (BLOCK, 128), 1)
    packed = jnp.zeros((BLOCK, 128), f32)
    for place, column in enumerate(columns):
        packed = jnp.where(lane == place, column, packed)
    return packed.T[0:STAT_ROWS, :]


def turn(values, cos_ref, low_ref, high_ref, rows, sign):
    parts = []
    for start in range(0, values.shape[1], 128):
        part = values[:, start : start + 128]
        swapped = pltpu.roll(part, 96, 1) * low_ref[rows, :] + pltpu.roll(part, 32, 1) * high_ref[
            rows, :
        ]
        parts.append(part * cos_ref[rows, :] + sign * swapped)
    return jnp.concatenate(parts, axis=1)


def head_only(values, head):
    lane = lax.broadcasted_iota(jnp.int32, values.shape, 1)
    inside = (lane >= head * HEAD_DIM) & (lane < (head + 1) * HEAD_DIM)
    return jnp.where(inside, values.astype(f32), 0.0).astype(bf16)


def send_tail(send, slots, first, second):
    lanes = send.shape[1]
    pieces = [row[:, start : start + lanes] for row in (first, second) for start in range(0, slots, lanes)]
    if len(pieces) < TAIL:
        pieces.append(jnp.zeros((TAIL - len(pieces), lanes), f32))
    send[slots : slots + TAIL, :] = jnp.concatenate(pieces, axis=0).astype(bf16)


def attend_kernel(place_ref, lengths, *refs, seq, count, width, heads, slots, full):
    pieces = refs[:count]
    gain, weight, cos_ref, low_ref, high_ref = refs[count : count + 5]
    normed, q_out, k_out, v_out, attended, log_sum, stats, keep, send = refs[count + 5 : count + 14]
    values_t, out_t = refs[count + 14 :]
    index = place_ref[0]
    length = lengths[seq]
    live = pl.cdiv(length, BLOCK)
    blocks = slots // BLOCK

    def project(block, carry):
        rows = block_rows(block)
        units, mean, factor = norm_parts([piece[rows, :].astype(f32) for piece in pieces], full)
        for place, unit in enumerate(units):
            gained = unit * gain[pl.ds(index ^ place, 1), :]
            normed[rows, feature_block(index, place, width)] = gained.astype(bf16)
        stats[:, rows] = columns_to_rows((mean, factor))
        row = normed[rows, :]
        turned = turn(dot_nn(row, weight[0]), cos_ref, low_ref, high_ref, rows, 1.0)
        q_out[rows, :] = (turned.astype(bf16).astype(f32) * HEAD_DIM**-0.5).astype(bf16)
        turned = turn(dot_nn(row, weight[1]), cos_ref, low_ref, high_ref, rows, 1.0)
        k_out[rows, :] = turned.astype(bf16)
        v_out[rows, :] = dot_nn(row, weight[2]).astype(bf16)
        return carry

    def clear(block, carry):
        rows = block_rows(block)
        normed[rows, :] = jnp.zeros((BLOCK, full), bf16)
        for ref in (q_out, k_out, v_out, attended):
            ref[rows, :] = jnp.zeros((BLOCK, width), bf16)
        stats[:, rows] = jnp.zeros((STAT_ROWS, BLOCK), f32)
        keep[rows, :] = jnp.zeros((BLOCK, keep.shape[1]), bf16)
        send[rows, :] = jnp.zeros((BLOCK, send.shape[1]), bf16)
        return carry

    lax.fori_loop(0, live, project, 0)
    lax.fori_loop(live, blocks, clear, 0)
    log_sum[...] = jnp.zeros(log_sum.shape, f32)

    def attend(count_live):
        span = count_live * BLOCK
        values_t[:, 0:span] = v_out[0:span, :].T

        def query_block(block, carry):
            rows = block_rows(block)
            queries = q_out[rows, :]
            for head in range(heads):
                mine = slice(head * HEAD_DIM, (head + 1) * HEAD_DIM)
                scores = dot_nt(k_out[0:span, :], head_only(queries, head))
                slot = lax.broadcasted_iota(jnp.int32, (span, BLOCK), 0)
                scores = jnp.where(slot < length, scores, masked_score)
                top = jnp.max(scores, axis=0, keepdims=True)
                weights = jnp.exp(scores - top)
                total = jnp.sum(weights, axis=0, keepdims=True)
                result = dot_nn(values_t[mine, 0:span], weights.astype(bf16))
                out_t[mine, :] = result * (1.0 / total)
                log_sum[head : head + 1, rows] = top + jnp.log(total)
            attended[rows, :] = out_t[...].T.astype(bf16)
            return carry

        lax.fori_loop(0, count_live, query_block, 0)

    for count_live in range(1, blocks + 1):
        pl.when(live == count_live)(functools.partial(attend, count_live))

    def output(block, carry):
        rows = block_rows(block)
        row = attended[rows, :]
        for place in range(count):
            part = dot_nt(row, weight[3, feature_block(index, place, width), :])
            target = slice((place // 2) * width, (place // 2 + 1) * width)
            if place % 2:
                send[rows, target] = part.astype(bf16)
            else:
                keep[rows, target] = part.astype(bf16)
        return carry

    lax.fori_loop(0, live, output, 0)


def mlp_kernel(place_ref, lengths, *refs, seq, count, width, slots, full):
    rows_in = refs[:count]
    grads_in = refs[count : 2 * count]
    gain, weight = refs[2 * count : 2 * count + 2]
    (normed, grads, mixed, grad_expanded, stats, out_keep, out_send, back_keep, back_send, kept) = (
        refs[2 * count + 2 :]
    )
    index = place_ref[0]
    length = lengths[seq]
    block = pl.program_id(0)
    rows = block_rows(block)

    @pl.when(block * BLOCK < length)
    def _():
        slot = block * BLOCK + lax.broadcasted_iota(jnp.int32, (BLOCK, 1), 0)
        units, mean, factor = norm_parts([piece[...].astype(f32) for piece in rows_in], full)
        for place, unit in enumerate(units):
            here = feature_block(index, place, width)
            gained = unit * gain[pl.ds(index ^ place, 1), :]
            normed[:, here] = gained.astype(bf16)
            grad = jnp.where(slot < length, grads_in[place][...].astype(f32), 0.0)
            grads[:, here] = grad.astype(bf16)
        row = normed[...]
        grad = grads[...]
        gate = dot_nn(row, weight[0])
        linear = dot_nn(row, weight[1])
        grad_mixed = dot_nn(grad, weight[2])
        phi = 0.5 + 0.5 * lax.erf(gate * (0.5**0.5))
        activated = gate * phi
        density = jnp.exp(-0.5 * gate * gate) * (0.5 / jnp.pi) ** 0.5
        mixed_low = (activated * linear).astype(bf16)
        mixed[...] = mixed_low
        first = (grad_mixed * linear * (phi + gate * density)).astype(bf16)
        second = (grad_mixed * activated).astype(bf16)
        grad_expanded[0] = first
        grad_expanded[1] = second
        plain_sum = jnp.zeros((BLOCK, 1), f32)
        unit_sum = jnp.zeros((BLOCK, 1), f32)
        for place in range(count):
            here = feature_block(index, place, width)
            target = slice((place // 2) * width, (place // 2 + 1) * width)
            part = dot_nt(mixed_low, weight[2, here, :])
            back = dot_nt(first, weight[0, here, :]) + dot_nt(second, weight[1, here, :])
            plain_sum += jnp.sum(back * gain[pl.ds(index ^ place, 1), :], axis=-1, keepdims=True)
            unit_sum += jnp.sum(back * normed[:, here].astype(f32), axis=-1, keepdims=True)
            if place % 2:
                out_send[:, target] = part.astype(bf16)
                back_send[rows, target] = back.astype(bf16)
            else:
                out_keep[:, target] = part.astype(bf16)
                back_keep[:, target] = back.astype(bf16)
        lines = columns_to_rows((mean, factor, plain_sum, unit_sum))
        stats[...] = lines
        kept[:, rows] = lines

    @pl.when(block * BLOCK >= length)
    def _():
        for ref in (normed, grads, mixed, out_keep, out_send, back_keep, grad_expanded, stats):
            ref[...] = jnp.zeros(ref.shape, ref.dtype)
        back_send[rows, :] = jnp.zeros((BLOCK, back_send.shape[1]), bf16)
        kept[:, rows] = jnp.zeros((STAT_ROWS, BLOCK), f32)

    @pl.when(block == pl.num_programs(0) - 1)
    def _():
        send_tail(back_send, slots, kept[2:3, :], kept[3:4, :])


def attend_back_kernel(place_ref, lengths, *refs, seq, count, width, heads, slots, full):
    grads_in = refs[:count]
    (q_in, k_in, v_in, attended, log_sum, normed, gain, weight, cos_ref, low_ref, high_ref) = refs[
        count : count + 11
    ]
    grads, grad_projected, stats, keep, send = refs[count + 11 : count + 16]
    (grad_att, delta, keys_t, probs_all, scores_all, query_t, key_total, value_total) = refs[
        count + 16 :
    ]
    index = place_ref[0]
    length = lengths[seq]
    live = pl.cdiv(length, BLOCK)
    blocks = slots // BLOCK

    def enter(block, carry):
        rows = block_rows(block)
        for place in range(count):
            grads[rows, feature_block(index, place, width)] = grads_in[place][rows, :]
        grad = dot_nn(grads[rows, :], weight[3]).astype(bf16)
        grad_att[rows, :] = grad
        inner = (grad.astype(f32) * attended[rows, :].astype(f32)).T
        for head in range(heads):
            mine = slice(head * HEAD_DIM, (head + 1) * HEAD_DIM)
            delta[head : head + 1, rows] = jnp.sum(inner[mine, :], axis=0, keepdims=True)
        return carry

    def clear(block, carry):
        rows = block_rows(block)
        grads[rows, :] = jnp.zeros((BLOCK, full), bf16)
        for place in range(3):
            grad_projected[place, rows, :] = jnp.zeros((BLOCK, width), bf16)
        stats[:, rows] = jnp.zeros((STAT_ROWS, BLOCK), f32)
        keep[rows, :] = jnp.zeros((BLOCK, keep.shape[1]), bf16)
        send[rows, :] = jnp.zeros((BLOCK, send.shape[1]), bf16)
        return carry

    lax.fori_loop(0, live, enter, 0)
    lax.fori_loop(live, blocks, clear, 0)

    def attend(count_live):
        span = count_live * BLOCK
        keys_t[:, 0:span] = k_in[0:span, :].T
        key_total[0:span, :] = jnp.zeros((span, width), f32)
        value_total[0:span, :] = jnp.zeros((span, width), f32)

        def query_block(block, carry):
            rows = block_rows(block)
            queries = [head_only(q_in[rows, :], head) for head in range(heads)]
            grad_rows = [head_only(grad_att[rows, :], head) for head in range(heads)]
            for head in range(heads):
                mine = slice(head * HEAD_DIM, (head + 1) * HEAD_DIM)
                lanes = slice(head * BLOCK, (head + 1) * BLOCK)
                scores = dot_nt(k_in[0:span, :], queries[head])
                slot = lax.broadcasted_iota(jnp.int32, (span, BLOCK), 0)
                scores = jnp.where(slot < length, scores, masked_score)
                weights = jnp.exp(scores - log_sum[head : head + 1, rows])
                grad_weights = dot_nt(v_in[0:span, :], grad_rows[head])
                grad_scores = (weights * (grad_weights - delta[head : head + 1, rows])).astype(bf16)
                probs_all[0:span, lanes] = weights.astype(bf16)
                scores_all[0:span, lanes] = grad_scores
                query_t[mine, :] = dot_nn(keys_t[mine, 0:span], grad_scores)
            value_total[0:span, :] += dot_nn(probs_all[0:span, :], jnp.concatenate(grad_rows, axis=0))
            key_total[0:span, :] += dot_nn(scores_all[0:span, :], jnp.concatenate(queries, axis=0))
            turned = turn(query_t[...].T * HEAD_DIM**-0.5, cos_ref, low_ref, high_ref, rows, -1.0)
            grad_projected[0, rows, :] = turned.astype(bf16)
            return carry

        lax.fori_loop(0, count_live, query_block, 0)

    for count_live in range(1, blocks + 1):
        pl.when(live == count_live)(functools.partial(attend, count_live))

    def leave(block, carry):
        rows = block_rows(block)
        turned = turn(key_total[rows, :], cos_ref, low_ref, high_ref, rows, -1.0)
        grad_projected[1, rows, :] = turned.astype(bf16)
        grad_projected[2, rows, :] = value_total[rows, :].astype(bf16)
        plain_sum = jnp.zeros((BLOCK, 1), f32)
        unit_sum = jnp.zeros((BLOCK, 1), f32)
        for place in range(count):
            here = feature_block(index, place, width)
            target = slice((place // 2) * width, (place // 2 + 1) * width)
            back = sum(
                dot_nt(grad_projected[kind, rows, :], weight[kind, here, :]) for kind in range(3)
            )
            plain_sum += jnp.sum(back * gain[pl.ds(index ^ place, 1), :], axis=-1, keepdims=True)
            unit_sum += jnp.sum(back * normed[rows, here].astype(f32), axis=-1, keepdims=True)
            if place % 2:
                send[rows, target] = back.astype(bf16)
            else:
                keep[rows, target] = back.astype(bf16)
        zero = jnp.zeros((BLOCK, 1), f32)
        stats[:, rows] = columns_to_rows((zero, zero, plain_sum, unit_sum))
        return carry

    lax.fori_loop(0, live, leave, 0)
    send_tail(send, slots, stats[2:3, :], stats[3:4, :])


def rows_to_columns(rows):
    filler = jnp.zeros((128 - len(rows), rows[0].shape[1]), f32)
    return jnp.concatenate([*rows, filler], axis=0).T


def read_tail(tail, slots):
    values = tail[...].astype(f32)
    lanes = values.shape[1]
    lines = slots // lanes
    return [
        jnp.concatenate([values[row : row + 1] for row in range(start, start + lines)], axis=1)
        for start in (0, lines)
    ]


def near_kernel(*refs, blocks, terms, width, slots, tailed):
    parts = refs[: blocks * terms]
    going = refs[blocks * terms + 2 * tailed]
    step = pl.program_id(0)
    here = pl.ds(pl.multiple_of(step * GLUE, GLUE), GLUE)
    for block in range(blocks):
        total = sum(ref[...].astype(f32) for ref in parts[block * terms : (block + 1) * terms])
        going[here, block * width : (block + 1) * width] = total.astype(bf16)
    if tailed:
        tail, sums = refs[blocks * terms : blocks * terms + 2]
        sums_out = refs[-1]

        @pl.when(step == 0)
        def _():
            plain, unit = read_tail(tail, slots)
            plain = plain + sums[2:3, :]
            unit = unit + sums[3:4, :]
            empty = jnp.zeros((2, slots), f32)
            sums_out[...] = jnp.concatenate([empty, plain, unit, empty, empty], axis=0)
            send_tail(going, slots, plain, unit)


def residual_kernel(inputs, *refs):
    *terms, out, low = refs
    total = inputs[...].astype(f32) + sum(term[...].astype(f32) for term in terms)
    out[...] = total
    low[...] = total.astype(bf16)


def output_kernel(place_ref, lengths, residual, *refs, seq, terms):
    out = refs[-1]
    slot = pl.program_id(0) * GLUE + lax.broadcasted_iota(jnp.int32, (GLUE, 1), 0)
    total = residual[...] + sum(term[...].astype(f32) for term in refs[:terms])
    out[...] = jnp.where(slot < lengths[seq], total, 0.0)


def norm_back_kernel(place_ref, lengths, *refs, seq, terms, slots, full, masked):
    parts = refs[:terms]
    (tail, sums, stats, source, base, gain) = refs[terms : terms + 6]
    low = refs[-2] if masked else None
    out = refs[-3] if masked else refs[-2]
    gain_grad = refs[-1]
    step = pl.program_id(0)
    plain, unit_sum = read_tail(tail, slots)
    here = pl.ds(pl.multiple_of(step * GLUE, GLUE), GLUE)
    columns = rows_to_columns([stats[0:1, here], stats[1:2, here], sums[2:3, here], sums[3:4, here]])
    lane_block = [plain[:, start : start + GLUE] for start in range(0, slots, GLUE)]
    unit_block = [unit_sum[:, start : start + GLUE] for start in range(0, slots, GLUE)]
    more_plain = lane_block[0]
    more_unit = unit_block[0]
    for place in range(1, len(lane_block)):
        more_plain = jnp.where(step == place, lane_block[place], more_plain)
        more_unit = jnp.where(step == place, unit_block[place], more_unit)
    more = rows_to_columns([more_plain, more_unit])
    mean, factor = columns[:, 0:1], columns[:, 1:2]
    plain_mean = (columns[:, 2:3] + more[:, 0:1]) / full
    unit_mean = (columns[:, 3:4] + more[:, 1:2]) / full
    unit = (source[...].astype(f32) - mean) * factor
    gradient = sum(part[...].astype(f32) for part in parts)
    inner = gradient * gain[pl.ds(place_ref[0], 1), :] - plain_mean - unit * unit_mean
    below = base[...].astype(f32)
    if masked:
        slot = step * GLUE + lax.broadcasted_iota(jnp.int32, (GLUE, 1), 0)
        below = jnp.where(slot < lengths[seq], below, 0.0)
    total = below + factor * inner
    out[...] = total
    if masked:
        low[...] = total.astype(bf16)

    @pl.when(step == 0)
    def _():
        gain_grad[...] = jnp.zeros(gain_grad.shape, f32)

    gain_grad[0:1, :] += jnp.sum(gradient * unit, axis=0, keepdims=True)


def grad_kernel(*refs, pairs, seq_count):
    out = refs[-1]
    place = 0
    cursor = 0
    for kinds in pairs:
        lefts = refs[cursor : cursor + seq_count]
        rights = refs[cursor + seq_count : cursor + 2 * seq_count]
        cursor += 2 * seq_count
        for kind in range(kinds):
            total = sum(dot_tn(left[...], right[kind]) for left, right in zip(lefts, rights))
            for step in range(out.shape[0]):
                rows = out.shape[2]
                out[step, place] = total[step * rows : (step + 1) * rows, :].astype(bf16)
            place += 1


def weight_grads(groups, wide_count, full, micros, earlier):
    rows = full // wide_count
    per_step = max(BLOCK // rows, 1)
    columns = groups[0][1][0].shape[2]
    slots = groups[0][0][0].shape[0]
    seq_count = len(groups[0][0])
    pairs = tuple(rights[0].shape[0] for _, rights in groups)
    operands = []
    specs = []
    for lefts, rights in groups:
        for left in lefts:
            operands.append(left)
            specs.append(pl.BlockSpec((slots, rows * per_step), lambda step: (0, step)))
        for right in rights:
            operands.append(right)
            specs.append(pl.BlockSpec(right.shape, lambda step: (0, 0, 0)))
    kinds = sum(pairs)
    body = functools.partial(grad_kernel, pairs=pairs, seq_count=seq_count)
    body, operands, specs = after(body, operands, specs, earlier, 0)
    return pl.pallas_call(
        body,
        grid=(wide_count // per_step,),
        in_specs=specs,
        out_specs=pl.BlockSpec((per_step, kinds, rows, columns), lambda step: (step, 0, 0, 0)),
        out_shape=jax.ShapeDtypeStruct((wide_count, kinds, rows, columns), bf16),
        cost_estimate=estimate(micros),
    )(*operands)


def whole(shape):
    return pl.BlockSpec(shape, lambda step, *scalars: (0,) * len(shape))


def striped(columns, seq=0, blocks=0, column=0, rows=GLUE):
    return pl.BlockSpec((rows, columns), lambda step, *scalars: (seq * blocks + step, column))


def tail_spec(columns, slots):
    return pl.BlockSpec((TAIL, columns), lambda step, *scalars: (slots // TAIL, 0))


def after(body, operands, specs, earlier, scalars):
    place = scalars + len(operands)

    def ordered(*refs):
        return body(*refs[:place], *refs[place + len(earlier) :])

    unread = [pl.BlockSpec(memory_space=pl.ANY)] * len(earlier)
    return ordered, [*operands, *earlier], [*specs, *unread]


def estimate(micros):
    return pl.CostEstimate(flops=int(micros * 1e9), transcendentals=0, bytes_accessed=1 << 20)


def glue_call(body, scalars, operands, specs, outs, out_specs, steps, aliases=()):
    return pl.pallas_call(
        body,
        grid_spec=pltpu.PrefetchScalarGridSpec(
            num_scalar_prefetch=len(scalars), grid=(steps,), in_specs=specs, out_specs=out_specs
        ),
        out_shape=[jax.ShapeDtypeStruct(shape, kind) for shape, kind in outs],
        input_output_aliases=dict(aliases),
        cost_estimate=estimate(2),
    )(*scalars, *operands)


def call_kernel(
    body, meta, operands, specs, outs, scratch, micros, earlier, steps=1, out_specs=None
):
    body, operands, specs = after(body, operands, specs, earlier, 2)
    return pl.pallas_call(
        body,
        grid_spec=pltpu.PrefetchScalarGridSpec(
            num_scalar_prefetch=2,
            grid=(steps,),
            in_specs=specs,
            out_specs=out_specs or [whole(shape) for shape, _ in outs],
            scratch_shapes=scratch,
        ),
        out_shape=[jax.ShapeDtypeStruct(shape, kind) for shape, kind in outs],
        cost_estimate=estimate(micros),
    )(*meta, *operands)


def swap(values, distance, count):
    return lax.ppermute(values, "narrow", [(place, place ^ distance) for place in range(count)])


def gather_narrow(own, count):
    pieces = {0: own}
    distance = count // 2
    while distance:
        for place in sorted(pieces):
            pieces[place | distance] = swap(pieces[place], distance, count)
        distance //= 2
    return [pieces[place] for place in range(count)]


def reduce_narrow(keep, send, sums, count, width):
    slots = keep.shape[0]
    tailed = sums is not None
    received = swap(send, 1, count)
    terms = [(keep, 1), (received, 1)]
    blocks = count // 2
    distance = 2
    while distance < count:
        blocks //= 2
        operands = []
        specs = []
        for block in range(blocks):
            for term, stride in terms:
                operands.append(term)
                specs.append(striped(width, column=(2 * block + 1) * stride))
        lanes = blocks * width
        outs = [((slots + TAIL * tailed, lanes), bf16)]
        if tailed:
            operands += [received, sums]
            specs += [tail_spec(received.shape[1], slots), whole(sums.shape)]
            outs.append((sums.shape, f32))
        body = functools.partial(
            near_kernel, blocks=blocks, terms=len(terms), width=width, slots=slots, tailed=tailed
        )
        going, *rest = glue_call(
            body, (), operands, specs, outs, [whole(shape) for shape, _ in outs], slots // GLUE
        )
        if tailed:
            sums = rest[0]
        received = swap(going, distance, count)
        terms = [(term, 2 * stride) for term, stride in terms] + [(received, 1)]
        distance *= 2
    return [term for term, _ in terms], sums


def rotary_rows(slots):
    half = HEAD_DIM // 2
    inverse = theta_base ** (-2.0 * jnp.arange(half, dtype=f32) / HEAD_DIM)
    angles = jnp.arange(slots, dtype=f32)[:, None] * inverse[None, :]
    cos = jnp.cos(angles)
    sin = jnp.sin(angles)
    none = jnp.zeros_like(sin)
    copies = 128 // HEAD_DIM
    return (
        jnp.tile(jnp.concatenate([cos, cos], axis=1), (1, copies)),
        jnp.tile(jnp.concatenate([-sin, none], axis=1), (1, copies)),
        jnp.tile(jnp.concatenate([none, sin], axis=1), (1, copies)),
    )


def shards(
    inputs,
    lengths,
    attn_gain,
    attn_in_weight,
    attn_out_weight,
    mlp_gain,
    mlp_in_weight,
    mlp_out_weight,
    cotangent,
):
    count = lax.axis_size("narrow")
    wide_count = lax.axis_size("wide")
    index = lax.axis_index("narrow").astype(jnp.int32)
    tokens, width = inputs.shape
    full = width * count
    seq_count = lengths.shape[0]
    slots = tokens // seq_count
    heads = width // HEAD_DIM
    hidden = mlp_in_weight.shape[2]
    half = count // 2 * width
    tables = rotary_rows(slots)
    seqs = range(seq_count)
    blocks = slots // GLUE
    meta = (index.reshape(1), lengths)

    attn_weight = lax.all_gather(
        jnp.concatenate([attn_in_weight, attn_out_weight.T[None]]), "wide", axis=1, tiled=True
    )
    mlp_weight = lax.all_gather(
        jnp.concatenate([mlp_in_weight, mlp_out_weight.T[None]]), "wide", axis=1, tiled=True
    )
    input_pieces = gather_narrow(inputs, count)
    grad_pieces = gather_narrow(cotangent, count)
    attn_gain_rows = attn_gain.reshape(count, width)
    mlp_gain_rows = mlp_gain.reshape(count, width)

    def seq_spec(seq):
        return pl.BlockSpec((slots, width), lambda step, *scalars: (seq, 0))

    row_spec = whole((slots, width))
    table_specs = [whole((slots, 128))] * 3
    gain_spec = whole((count, width))
    attn_spec = whole(attn_weight.shape)
    sizes = dict(count=count, width=width, slots=slots, full=full)

    def forward_call(seq, earlier):
        return call_kernel(
            functools.partial(attend_kernel, seq=seq, heads=heads, **sizes),
            meta,
            [*input_pieces, attn_gain_rows, attn_weight, *tables],
            [seq_spec(seq)] * count + [gain_spec, attn_spec] + table_specs,
            [((slots, full), bf16)]
            + [((slots, width), bf16)] * 4
            + [((max(heads, STAT_ROWS), slots), f32), ((STAT_ROWS, slots), f32)]
            + [((slots, half), bf16), ((slots, half), bf16)],
            [pltpu.VMEM((width, slots), bf16), pltpu.VMEM((width, BLOCK), f32)],
            24,
            earlier,
        )

    def middle_call(seq, earlier):
        return call_kernel(
            functools.partial(mlp_kernel, seq=seq, **sizes),
            meta,
            [*residual_pieces[seq], *grad_pieces, mlp_gain_rows, mlp_weight],
            [striped(width, rows=BLOCK)] * count
            + [striped(width, seq, slots // BLOCK, rows=BLOCK)] * count
            + [gain_spec, whole(mlp_weight.shape)],
            [((slots, full), bf16), ((slots, full), bf16), ((slots, hidden), bf16)]
            + [((2, slots, hidden), bf16), ((STAT_ROWS, slots), f32)]
            + [((slots, half), bf16)] * 3
            + [((slots + TAIL, half), bf16)],
            [pltpu.VMEM((STAT_ROWS, slots), f32)],
            20,
            earlier,
            slots // BLOCK,
            [striped(full, rows=BLOCK)] * 2
            + [striped(hidden, rows=BLOCK)]
            + [pl.BlockSpec((2, BLOCK, hidden), lambda step, *scalars: (0, step, 0))]
            + [pl.BlockSpec((STAT_ROWS, BLOCK), lambda step, *scalars: (0, step))]
            + [striped(half, rows=BLOCK)] * 3
            + [whole((slots + TAIL, half))],
        )

    def backward_call(seq, earlier):
        normed, queries, keys, values, attended, log_sum = forward[seq][:6]
        return call_kernel(
            functools.partial(attend_back_kernel, seq=seq, heads=heads, **sizes),
            meta,
            [*attn_grad_pieces[seq], queries, keys, values, attended, log_sum, normed]
            + [attn_gain_rows, attn_weight, *tables],
            [row_spec] * (count + 4)
            + [whole(log_sum.shape), whole((slots, full)), gain_spec, attn_spec]
            + table_specs,
            [((slots, full), bf16), ((3, slots, width), bf16), ((STAT_ROWS, slots), f32)]
            + [((slots, half), bf16), ((slots + TAIL, half), bf16)],
            [
                pltpu.VMEM((slots, width), bf16),
                pltpu.VMEM((max(heads, STAT_ROWS), slots), f32),
                pltpu.VMEM((width, slots), bf16),
                pltpu.VMEM((slots, heads * BLOCK), bf16),
                pltpu.VMEM((slots, heads * BLOCK), bf16),
                pltpu.VMEM((width, BLOCK), f32),
                pltpu.VMEM((slots, width), f32),
                pltpu.VMEM((slots, width), f32),
            ],
            26,
            earlier,
        )

    def norm_back_call(seq, parts, source, base, gains, target=None):
        terms, sums, stats = parts
        masked = target is None
        target = target or []
        outs = [((slots, width), f32), ((slots, width), bf16)]
        out_specs = [striped(width)] * 2
        if not masked:
            outs = [((tokens, width), f32)]
            out_specs = [striped(width, seq, blocks)]
        return glue_call(
            functools.partial(
                norm_back_kernel, seq=seq, terms=len(terms), slots=slots, full=full, masked=masked
            ),
            meta,
            [*terms, terms[-1], sums, stats, source[0], base[0], gains, *target],
            [striped(width)] * len(terms)
            + [tail_spec(width, slots)]
            + [whole(sums.shape), whole(stats.shape), source[1], base[1], gain_spec]
            + [pl.BlockSpec(memory_space=pl.ANY)] * len(target),
            [*outs, ((STAT_ROWS, width), f32)],
            [*out_specs, whole((STAT_ROWS, width))],
            blocks,
            [(8 + len(terms), 0)] * len(target),
        )

    forward, residuals, residual_pieces = [], [], []
    earlier = [grad_pieces[count // 2]]
    for seq in seqs:
        forward.append(forward_call(seq, earlier))
        earlier = [forward[seq][6]]
    for seq in seqs:
        terms, _ = reduce_narrow(forward[seq][7], forward[seq][8], None, count, width)
        residual, low = glue_call(
            residual_kernel,
            (),
            [inputs, *terms],
            [striped(width, seq, blocks)] + [striped(width)] * len(terms),
            [((slots, width), f32), ((slots, width), bf16)],
            [striped(width)] * 2,
            blocks,
        )
        residuals.append(residual)
        residual_pieces.append(gather_narrow(low, count))

    middle, grad_residuals, attn_grad_pieces = [], [], []
    mlp_gain_local = 0.0
    for seq in seqs:
        middle.append(middle_call(seq, earlier))
        earlier = [middle[seq][4]]
    for seq in seqs:
        terms, sums = reduce_narrow(middle[seq][7], middle[seq][8], middle[seq][4], count, width)
        grad_residual, low, gain_part = norm_back_call(
            seq,
            (terms, sums, middle[seq][4]),
            (residuals[seq], striped(width)),
            (cotangent, striped(width, seq, blocks)),
            mlp_gain_rows,
        )
        grad_residuals.append(grad_residual)
        mlp_gain_local = mlp_gain_local + gain_part[0]
        attn_grad_pieces.append(gather_narrow(low, count))
    mlp_grads = weight_grads(
        [
            ([middle[seq][0] for seq in seqs], [middle[seq][3] for seq in seqs]),
            ([middle[seq][1] for seq in seqs], [middle[seq][2][None] for seq in seqs]),
        ],
        wide_count,
        full,
        17,
        earlier,
    )
    mlp_shard = lax.psum_scatter(
        mlp_grads.reshape(-1, hidden), "wide", scatter_dimension=0, tiled=True
    )

    backward, output, inputs_grad = [], [], []
    earlier = [mlp_grads]
    for seq in seqs:
        backward.append(backward_call(seq, earlier))
        earlier = [backward[seq][2]]
    for seq in seqs:
        terms, _ = reduce_narrow(middle[seq][5], middle[seq][6], None, count, width)
        output = glue_call(
            functools.partial(output_kernel, seq=seq, terms=len(terms)),
            meta,
            [residuals[seq], *terms, *output],
            [striped(width)] * (1 + len(terms)) + [pl.BlockSpec(memory_space=pl.ANY)] * len(output),
            [((tokens, width), f32)],
            [striped(width, seq, blocks)],
            blocks,
            [(3 + len(terms), 0)] * len(output),
        )
    attn_grads = weight_grads(
        [
            ([forward[seq][0] for seq in seqs], [backward[seq][1] for seq in seqs]),
            ([backward[seq][0] for seq in seqs], [forward[seq][4][None] for seq in seqs]),
        ],
        wide_count,
        full,
        10,
        [*earlier, mlp_shard],
    )
    mlp_shard = mlp_shard.reshape(mlp_grads.shape[1:])
    attn_shard = lax.psum_scatter(
        attn_grads.reshape(-1, width), "wide", scatter_dimension=0, tiled=True
    ).reshape(attn_grads.shape[1:])

    attn_gain_local = 0.0
    for seq in seqs:
        terms, sums = reduce_narrow(
            backward[seq][3], backward[seq][4], backward[seq][2], count, width
        )
        *inputs_grad, gain_part = norm_back_call(
            seq,
            (terms, sums, forward[seq][6]),
            (inputs, striped(width, seq, blocks)),
            (grad_residuals[seq], striped(width)),
            attn_gain_rows,
            inputs_grad,
        )
        attn_gain_local = attn_gain_local + gain_part[0]
    gain_grads = lax.psum(jnp.stack([attn_gain_local, mlp_gain_local]), "wide")
    return (
        output[0],
        inputs_grad[0],
        gain_grads[0],
        attn_shard[:3].astype(f32),
        attn_shard[3].T.astype(f32),
        gain_grads[1],
        mlp_shard[:2].astype(f32),
        mlp_shard[2].T.astype(f32),
    )


def solution(mesh):
    in_specs = (
        P("wide", "narrow"),
        P("wide"),
        P(),
        P(None, "wide", "narrow"),
        P("narrow", "wide"),
        P(),
        P(None, "wide", "narrow"),
        P("narrow", "wide"),
        P("wide", "narrow"),
    )
    out_specs = (
        P("wide", "narrow"),
        P("wide", "narrow"),
        P("narrow"),
        P(None, "wide", "narrow"),
        P("narrow", "wide"),
        P("narrow"),
        P(None, "wide", "narrow"),
        P("narrow", "wide"),
    )
    return jax.shard_map(shards, mesh=mesh, in_specs=in_specs, out_specs=out_specs, check_vma=False)
```

```python
import functools

import jax
import jax.numpy as jnp
from jax import lax
from jax.experimental import pallas as pl
from jax.experimental.pallas import tpu as pltpu
from jax.sharding import PartitionSpec as P


HEAD_DIM = 64
epsilon = 1e-05
theta_base = 160000.0
masked_score = -1e30
BLOCK = 256
GLUE = 512
TAIL = 16
STAT_ROWS = 8
f32 = jnp.float32
bf16 = jnp.bfloat16


def dot_nn(left, right):
    return lax.dot_general(left, right, (((1,), (0,)), ((), ())), preferred_element_type=f32)


def dot_nt(left, right):
    return lax.dot_general(left, right, (((1,), (1,)), ((), ())), preferred_element_type=f32)


def dot_tn(left, right):
    return lax.dot_general(left, right, (((0,), (0,)), ((), ())), preferred_element_type=f32)


def block_rows(index):
    return pl.ds(pl.multiple_of(index * BLOCK, BLOCK), BLOCK)


def feature_block(index, distance, width):
    return pl.ds(pl.multiple_of((index ^ distance) * width, width), width)


def norm_parts(parts, full):
    mean = sum(jnp.sum(part, axis=-1, keepdims=True) for part in parts) / full
    parts = [part - mean for part in parts]
    spread = sum(jnp.sum(part * part, axis=-1, keepdims=True) for part in parts) / full
    factor = lax.rsqrt(spread + epsilon)
    return [part * factor for part in parts], mean, factor


def columns_to_rows(columns):
    lane = lax.broadcasted_iota(jnp.int32, (BLOCK, 128), 1)
    packed = jnp.zeros((BLOCK, 128), f32)
    for place, column in enumerate(columns):
        packed = jnp.where(lane == place, column, packed)
    return packed.T[0:STAT_ROWS, :]


def turn(values, cos_ref, low_ref, high_ref, rows, sign):
    parts = []
    for start in range(0, values.shape[1], 128):
        part = values[:, start : start + 128]
        swapped = pltpu.roll(part, 96, 1) * low_ref[rows, :] + pltpu.roll(part, 32, 1) * high_ref[
            rows, :
        ]
        parts.append(part * cos_ref[rows, :] + sign * swapped)
    return jnp.concatenate(parts, axis=1)


def head_only(values, head):
    lane = lax.broadcasted_iota(jnp.int32, values.shape, 1)
    inside = (lane >= head * HEAD_DIM) & (lane < (head + 1) * HEAD_DIM)
    return jnp.where(inside, values.astype(f32), 0.0).astype(bf16)


def send_tail(send, slots, first, second):
    lanes = send.shape[1]
    pieces = [row[:, start : start + lanes] for row in (first, second) for start in range(0, slots, lanes)]
    if len(pieces) < TAIL:
        pieces.append(jnp.zeros((TAIL - len(pieces), lanes), f32))
    send[slots : slots + TAIL, :] = jnp.concatenate(pieces, axis=0).astype(bf16)


def attend_kernel(place_ref, lengths, *refs, seq, count, width, heads, slots, full):
    pieces = refs[:count]
    gain, weight, cos_ref, low_ref, high_ref = refs[count : count + 5]
    normed, q_out, k_out, v_out, attended, log_sum, stats, keep, send = refs[count + 5 : count + 14]
    values_t, out_t = refs[count + 14 :]
    index = place_ref[0]
    length = lengths[seq]
    live = pl.cdiv(length, BLOCK)
    blocks = slots // BLOCK

    def project(block, carry):
        rows = block_rows(block)
        units, mean, factor = norm_parts([piece[rows, :].astype(f32) for piece in pieces], full)
        for place, unit in enumerate(units):
            gained = unit * gain[pl.ds(index ^ place, 1), :]
            normed[rows, feature_block(index, place, width)] = gained.astype(bf16)
        stats[:, rows] = columns_to_rows((mean, factor))
        row = normed[rows, :]
        turned = turn(dot_nn(row, weight[0]), cos_ref, low_ref, high_ref, rows, 1.0)
        q_out[rows, :] = (turned.astype(bf16).astype(f32) * HEAD_DIM**-0.5).astype(bf16)
        turned = turn(dot_nn(row, weight[1]), cos_ref, low_ref, high_ref, rows, 1.0)
        k_out[rows, :] = turned.astype(bf16)
        v_out[rows, :] = dot_nn(row, weight[2]).astype(bf16)
        return carry

    def clear(block, carry):
        rows = block_rows(block)
        normed[rows, :] = jnp.zeros((BLOCK, full), bf16)
        for ref in (q_out, k_out, v_out, attended):
            ref[rows, :] = jnp.zeros((BLOCK, width), bf16)
        stats[:, rows] = jnp.zeros((STAT_ROWS, BLOCK), f32)
        keep[rows, :] = jnp.zeros((BLOCK, keep.shape[1]), bf16)
        send[rows, :] = jnp.zeros((BLOCK, send.shape[1]), bf16)
        return carry

    lax.fori_loop(0, live, project, 0)
    lax.fori_loop(live, blocks, clear, 0)
    log_sum[...] = jnp.zeros(log_sum.shape, f32)

    def attend(count_live):
        span = count_live * BLOCK
        values_t[:, 0:span] = v_out[0:span, :].T

        def query_block(block, carry):
            rows = block_rows(block)
            queries = q_out[rows, :]
            for head in range(heads):
                mine = slice(head * HEAD_DIM, (head + 1) * HEAD_DIM)
                scores = dot_nt(k_out[0:span, :], head_only(queries, head))
                slot = lax.broadcasted_iota(jnp.int32, (span, BLOCK), 0)
                scores = jnp.where(slot < length, scores, masked_score)
                top = jnp.max(scores, axis=0, keepdims=True)
                weights = jnp.exp(scores - top)
                total = jnp.sum(weights, axis=0, keepdims=True)
                result = dot_nn(values_t[mine, 0:span], weights.astype(bf16))
                out_t[mine, :] = result * (1.0 / total)
                log_sum[head : head + 1, rows] = top + jnp.log(total)
            attended[rows, :] = out_t[...].T.astype(bf16)
            return carry

        lax.fori_loop(0, count_live, query_block, 0)

    for count_live in range(1, blocks + 1):
        pl.when(live == count_live)(functools.partial(attend, count_live))

    def output(block, carry):
        rows = block_rows(block)
        row = attended[rows, :]
        for place in range(count):
            part = dot_nt(row, weight[3, feature_block(index, place, width), :])
            target = slice((place // 2) * width, (place // 2 + 1) * width)
            if place % 2:
                send[rows, target] = part.astype(bf16)
            else:
                keep[rows, target] = part.astype(bf16)
        return carry

    lax.fori_loop(0, live, output, 0)


def mlp_kernel(place_ref, lengths, *refs, seq, count, width, slots, full):
    rows_in = refs[:count]
    grads_in = refs[count : 2 * count]
    gain, weight = refs[2 * count : 2 * count + 2]
    (normed, grads, mixed, grad_expanded, stats, out_keep, out_send, back_keep, back_send, kept) = (
        refs[2 * count + 2 :]
    )
    index = place_ref[0]
    length = lengths[seq]
    block = pl.program_id(0)
    rows = block_rows(block)

    @pl.when(block * BLOCK < length)
    def _():
        slot = block * BLOCK + lax.broadcasted_iota(jnp.int32, (BLOCK, 1), 0)
        units, mean, factor = norm_parts([piece[...].astype(f32) for piece in rows_in], full)
        for place, unit in enumerate(units):
            here = feature_block(index, place, width)
            gained = unit * gain[pl.ds(index ^ place, 1), :]
            normed[:, here] = gained.astype(bf16)
            grad = jnp.where(slot < length, grads_in[place][...].astype(f32), 0.0)
            grads[:, here] = grad.astype(bf16)
        row = normed[...]
        grad = grads[...]
        gate = dot_nn(row, weight[0])
        linear = dot_nn(row, weight[1])
        grad_mixed = dot_nn(grad, weight[2])
        phi = 0.5 + 0.5 * lax.erf(gate * (0.5**0.5))
        activated = gate * phi
        density = jnp.exp(-0.5 * gate * gate) * (0.5 / jnp.pi) ** 0.5
        mixed_low = (activated * linear).astype(bf16)
        mixed[...] = mixed_low
        first = (grad_mixed * linear * (phi + gate * density)).astype(bf16)
        second = (grad_mixed * activated).astype(bf16)
        grad_expanded[0] = first
        grad_expanded[1] = second
        plain_sum = jnp.zeros((BLOCK, 1), f32)
        unit_sum = jnp.zeros((BLOCK, 1), f32)
        for place in range(count):
            here = feature_block(index, place, width)
            target = slice((place // 2) * width, (place // 2 + 1) * width)
            part = dot_nt(mixed_low, weight[2, here, :])
            back = dot_nt(first, weight[0, here, :]) + dot_nt(second, weight[1, here, :])
            plain_sum += jnp.sum(back * gain[pl.ds(index ^ place, 1), :], axis=-1, keepdims=True)
            unit_sum += jnp.sum(back * normed[:, here].astype(f32), axis=-1, keepdims=True)
            if place % 2:
                out_send[:, target] = part.astype(bf16)
                back_send[rows, target] = back.astype(bf16)
            else:
                out_keep[:, target] = part.astype(bf16)
                back_keep[:, target] = back.astype(bf16)
        lines = columns_to_rows((mean, factor, plain_sum, unit_sum))
        stats[...] = lines
        kept[:, rows] = lines

    @pl.when(block * BLOCK >= length)
    def _():
        for ref in (normed, grads, mixed, out_keep, out_send, back_keep, grad_expanded, stats):
            ref[...] = jnp.zeros(ref.shape, ref.dtype)
        back_send[rows, :] = jnp.zeros((BLOCK, back_send.shape[1]), bf16)
        kept[:, rows] = jnp.zeros((STAT_ROWS, BLOCK), f32)

    @pl.when(block == pl.num_programs(0) - 1)
    def _():
        send_tail(back_send, slots, kept[2:3, :], kept[3:4, :])


def attend_back_kernel(place_ref, lengths, *refs, seq, count, width, heads, slots, full):
    grads_in = refs[:count]
    (q_in, k_in, v_in, attended, log_sum, normed, gain, weight, cos_ref, low_ref, high_ref) = refs[
        count : count + 11
    ]
    grads, grad_projected, stats, keep, send = refs[count + 11 : count + 16]
    (grad_att, delta, keys_t, probs_all, scores_all, query_t, key_total, value_total) = refs[
        count + 16 :
    ]
    index = place_ref[0]
    length = lengths[seq]
    live = pl.cdiv(length, BLOCK)
    blocks = slots // BLOCK

    def enter(block, carry):
        rows = block_rows(block)
        for place in range(count):
            grads[rows, feature_block(index, place, width)] = grads_in[place][rows, :]
        grad = dot_nn(grads[rows, :], weight[3]).astype(bf16)
        grad_att[rows, :] = grad
        inner = (grad.astype(f32) * attended[rows, :].astype(f32)).T
        for head in range(heads):
            mine = slice(head * HEAD_DIM, (head + 1) * HEAD_DIM)
            delta[head : head + 1, rows] = jnp.sum(inner[mine, :], axis=0, keepdims=True)
        return carry

    def clear(block, carry):
        rows = block_rows(block)
        grads[rows, :] = jnp.zeros((BLOCK, full), bf16)
        for place in range(3):
            grad_projected[place, rows, :] = jnp.zeros((BLOCK, width), bf16)
        stats[:, rows] = jnp.zeros((STAT_ROWS, BLOCK), f32)
        keep[rows, :] = jnp.zeros((BLOCK, keep.shape[1]), bf16)
        send[rows, :] = jnp.zeros((BLOCK, send.shape[1]), bf16)
        return carry

    lax.fori_loop(0, live, enter, 0)
    lax.fori_loop(live, blocks, clear, 0)

    def attend(count_live):
        span = count_live * BLOCK
        keys_t[:, 0:span] = k_in[0:span, :].T
        key_total[0:span, :] = jnp.zeros((span, width), f32)
        value_total[0:span, :] = jnp.zeros((span, width), f32)

        def query_block(block, carry):
            rows = block_rows(block)
            queries = [head_only(q_in[rows, :], head) for head in range(heads)]
            grad_rows = [head_only(grad_att[rows, :], head) for head in range(heads)]
            for head in range(heads):
                mine = slice(head * HEAD_DIM, (head + 1) * HEAD_DIM)
                lanes = slice(head * BLOCK, (head + 1) * BLOCK)
                scores = dot_nt(k_in[0:span, :], queries[head])
                slot = lax.broadcasted_iota(jnp.int32, (span, BLOCK), 0)
                scores = jnp.where(slot < length, scores, masked_score)
                weights = jnp.exp(scores - log_sum[head : head + 1, rows])
                grad_weights = dot_nt(v_in[0:span, :], grad_rows[head])
                grad_scores = (weights * (grad_weights - delta[head : head + 1, rows])).astype(bf16)
                probs_all[0:span, lanes] = weights.astype(bf16)
                scores_all[0:span, lanes] = grad_scores
                query_t[mine, :] = dot_nn(keys_t[mine, 0:span], grad_scores)
            value_total[0:span, :] += dot_nn(probs_all[0:span, :], jnp.concatenate(grad_rows, axis=0))
            key_total[0:span, :] += dot_nn(scores_all[0:span, :], jnp.concatenate(queries, axis=0))
            turned = turn(query_t[...].T * HEAD_DIM**-0.5, cos_ref, low_ref, high_ref, rows, -1.0)
            grad_projected[0, rows, :] = turned.astype(bf16)
            return carry

        lax.fori_loop(0, count_live, query_block, 0)

    for count_live in range(1, blocks + 1):
        pl.when(live == count_live)(functools.partial(attend, count_live))

    def leave(block, carry):
        rows = block_rows(block)
        turned = turn(key_total[rows, :], cos_ref, low_ref, high_ref, rows, -1.0)
        grad_projected[1, rows, :] = turned.astype(bf16)
        grad_projected[2, rows, :] = value_total[rows, :].astype(bf16)
        plain_sum = jnp.zeros((BLOCK, 1), f32)
        unit_sum = jnp.zeros((BLOCK, 1), f32)
        for place in range(count):
            here = feature_block(index, place, width)
            target = slice((place // 2) * width, (place // 2 + 1) * width)
            back = sum(
                dot_nt(grad_projected[kind, rows, :], weight[kind, here, :]) for kind in range(3)
            )
            plain_sum += jnp.sum(back * gain[pl.ds(index ^ place, 1), :], axis=-1, keepdims=True)
            unit_sum += jnp.sum(back * normed[rows, here].astype(f32), axis=-1, keepdims=True)
            if place % 2:
                send[rows, target] = back.astype(bf16)
            else:
                keep[rows, target] = back.astype(bf16)
        zero = jnp.zeros((BLOCK, 1), f32)
        stats[:, rows] = columns_to_rows((zero, zero, plain_sum, unit_sum))
        return carry

    lax.fori_loop(0, live, leave, 0)
    send_tail(send, slots, stats[2:3, :], stats[3:4, :])


def rows_to_columns(rows):
    filler = jnp.zeros((128 - len(rows), rows[0].shape[1]), f32)
    return jnp.concatenate([*rows, filler], axis=0).T


def read_tail(tail, slots):
    values = tail[...].astype(f32)
    lanes = values.shape[1]
    lines = slots // lanes
    return [
        jnp.concatenate([values[row : row + 1] for row in range(start, start + lines)], axis=1)
        for start in (0, lines)
    ]


def near_kernel(*refs, blocks, terms, width, slots, tailed):
    parts = refs[: blocks * terms]
    going = refs[blocks * terms + 2 * tailed]
    step = pl.program_id(0)
    here = pl.ds(pl.multiple_of(step * GLUE, GLUE), GLUE)
    for block in range(blocks):
        total = sum(ref[...].astype(f32) for ref in parts[block * terms : (block + 1) * terms])
        going[here, block * width : (block + 1) * width] = total.astype(bf16)
    if tailed:
        tail, sums = refs[blocks * terms : blocks * terms + 2]
        sums_out = refs[-1]

        @pl.when(step == 0)
        def _():
            plain, unit = read_tail(tail, slots)
            plain = plain + sums[2:3, :]
            unit = unit + sums[3:4, :]
            empty = jnp.zeros((2, slots), f32)
            sums_out[...] = jnp.concatenate([empty, plain, unit, empty, empty], axis=0)
            send_tail(going, slots, plain, unit)


def residual_kernel(inputs, *refs):
    *terms, out, low = refs
    total = inputs[...].astype(f32) + sum(term[...].astype(f32) for term in terms)
    out[...] = total
    low[...] = total.astype(bf16)


def output_kernel(place_ref, lengths, residual, *refs, seq, terms):
    out = refs[-1]
    slot = pl.program_id(0) * GLUE + lax.broadcasted_iota(jnp.int32, (GLUE, 1), 0)
    total = residual[...] + sum(term[...].astype(f32) for term in refs[:terms])
    out[...] = jnp.where(slot < lengths[seq], total, 0.0)


def norm_back_kernel(place_ref, lengths, *refs, seq, terms, slots, full, masked):
    parts = refs[:terms]
    (tail, sums, stats, source, base, gain) = refs[terms : terms + 6]
    low = refs[-2] if masked else None
    out = refs[-3] if masked else refs[-2]
    gain_grad = refs[-1]
    step = pl.program_id(0)
    plain, unit_sum = read_tail(tail, slots)
    here = pl.ds(pl.multiple_of(step * GLUE, GLUE), GLUE)
    columns = rows_to_columns([stats[0:1, here], stats[1:2, here], sums[2:3, here], sums[3:4, here]])
    lane_block = [plain[:, start : start + GLUE] for start in range(0, slots, GLUE)]
    unit_block = [unit_sum[:, start : start + GLUE] for start in range(0, slots, GLUE)]
    more_plain = lane_block[0]
    more_unit = unit_block[0]
    for place in range(1, len(lane_block)):
        more_plain = jnp.where(step == place, lane_block[place], more_plain)
        more_unit = jnp.where(step == place, unit_block[place], more_unit)
    more = rows_to_columns([more_plain, more_unit])
    mean, factor = columns[:, 0:1], columns[:, 1:2]
    plain_mean = (columns[:, 2:3] + more[:, 0:1]) / full
    unit_mean = (columns[:, 3:4] + more[:, 1:2]) / full
    unit = (source[...].astype(f32) - mean) * factor
    gradient = sum(part[...].astype(f32) for part in parts)
    inner = gradient * gain[pl.ds(place_ref[0], 1), :] - plain_mean - unit * unit_mean
    below = base[...].astype(f32)
    if masked:
        slot = step * GLUE + lax.broadcasted_iota(jnp.int32, (GLUE, 1), 0)
        below = jnp.where(slot < lengths[seq], below, 0.0)
    total = below + factor * inner
    out[...] = total
    if masked:
        low[...] = total.astype(bf16)

    @pl.when(step == 0)
    def _():
        gain_grad[...] = jnp.zeros(gain_grad.shape, f32)

    gain_grad[0:1, :] += jnp.sum(gradient * unit, axis=0, keepdims=True)


def grad_kernel(*refs, pairs, seq_count):
    out = refs[-1]
    place = 0
    cursor = 0
    for kinds in pairs:
        lefts = refs[cursor : cursor + seq_count]
        rights = refs[cursor + seq_count : cursor + 2 * seq_count]
        cursor += 2 * seq_count
        for kind in range(kinds):
            total = sum(dot_tn(left[...], right[kind]) for left, right in zip(lefts, rights))
            for step in range(out.shape[0]):
                rows = out.shape[2]
                out[step, place] = total[step * rows : (step + 1) * rows, :].astype(bf16)
            place += 1


def weight_grads(groups, wide_count, full, micros, earlier):
    rows = full // wide_count
    per_step = max(BLOCK // rows, 1)
    columns = groups[0][1][0].shape[2]
    slots = groups[0][0][0].shape[0]
    seq_count = len(groups[0][0])
    pairs = tuple(rights[0].shape[0] for _, rights in groups)
    operands = []
    specs = []
    for lefts, rights in groups:
        for left in lefts:
            operands.append(left)
            specs.append(pl.BlockSpec((slots, rows * per_step), lambda step: (0, step)))
        for right in rights:
            operands.append(right)
            specs.append(pl.BlockSpec(right.shape, lambda step: (0, 0, 0)))
    kinds = sum(pairs)
    body = functools.partial(grad_kernel, pairs=pairs, seq_count=seq_count)
    body, operands, specs = after(body, operands, specs, earlier, 0)
    return pl.pallas_call(
        body,
        grid=(wide_count // per_step,),
        in_specs=specs,
        out_specs=pl.BlockSpec((per_step, kinds, rows, columns), lambda step: (step, 0, 0, 0)),
        out_shape=jax.ShapeDtypeStruct((wide_count, kinds, rows, columns), bf16),
        cost_estimate=estimate(micros),
    )(*operands)


def whole(shape):
    return pl.BlockSpec(shape, lambda step, *scalars: (0,) * len(shape))


def striped(columns, seq=0, blocks=0, column=0, rows=GLUE):
    return pl.BlockSpec((rows, columns), lambda step, *scalars: (seq * blocks + step, column))


def tail_spec(columns, slots):
    return pl.BlockSpec((TAIL, columns), lambda step, *scalars: (slots // TAIL, 0))


def after(body, operands, specs, earlier, scalars):
    place = scalars + len(operands)

    def ordered(*refs):
        return body(*refs[:place], *refs[place + len(earlier) :])

    unread = [pl.BlockSpec(memory_space=pl.ANY)] * len(earlier)
    return ordered, [*operands, *earlier], [*specs, *unread]


def estimate(micros):
    return pl.CostEstimate(flops=int(micros * 1e9), transcendentals=0, bytes_accessed=1 << 20)


def glue_call(body, scalars, operands, specs, outs, out_specs, steps, aliases=()):
    return pl.pallas_call(
        body,
        grid_spec=pltpu.PrefetchScalarGridSpec(
            num_scalar_prefetch=len(scalars), grid=(steps,), in_specs=specs, out_specs=out_specs
        ),
        out_shape=[jax.ShapeDtypeStruct(shape, kind) for shape, kind in outs],
        input_output_aliases=dict(aliases),
        cost_estimate=estimate(2),
    )(*scalars, *operands)


def call_kernel(
    body, meta, operands, specs, outs, scratch, micros, earlier, steps=1, out_specs=None
):
    body, operands, specs = after(body, operands, specs, earlier, 2)
    return pl.pallas_call(
        body,
        grid_spec=pltpu.PrefetchScalarGridSpec(
            num_scalar_prefetch=2,
            grid=(steps,),
            in_specs=specs,
            out_specs=out_specs or [whole(shape) for shape, _ in outs],
            scratch_shapes=scratch,
        ),
        out_shape=[jax.ShapeDtypeStruct(shape, kind) for shape, kind in outs],
        cost_estimate=estimate(micros),
    )(*meta, *operands)


def swap(values, distance, count):
    return lax.ppermute(values, "narrow", [(place, place ^ distance) for place in range(count)])


def gather_narrow(own, count):
    pieces = {0: own}
    distance = count // 2
    while distance:
        for place in sorted(pieces):
            pieces[place | distance] = swap(pieces[place], distance, count)
        distance //= 2
    return [pieces[place] for place in range(count)]


def reduce_narrow(keep, send, sums, count, width):
    slots = keep.shape[0]
    tailed = sums is not None
    received = swap(send, 1, count)
    terms = [(keep, 1), (received, 1)]
    blocks = count // 2
    distance = 2
    while distance < count:
        blocks //= 2
        operands = []
        specs = []
        for block in range(blocks):
            for term, stride in terms:
                operands.append(term)
                specs.append(striped(width, column=(2 * block + 1) * stride))
        lanes = blocks * width
        outs = [((slots + TAIL * tailed, lanes), bf16)]
        if tailed:
            operands += [received, sums]
            specs += [tail_spec(received.shape[1], slots), whole(sums.shape)]
            outs.append((sums.shape, f32))
        body = functools.partial(
            near_kernel, blocks=blocks, terms=len(terms), width=width, slots=slots, tailed=tailed
        )
        going, *rest = glue_call(
            body, (), operands, specs, outs, [whole(shape) for shape, _ in outs], slots // GLUE
        )
        if tailed:
            sums = rest[0]
        received = swap(going, distance, count)
        terms = [(term, 2 * stride) for term, stride in terms] + [(received, 1)]
        distance *= 2
    return [term for term, _ in terms], sums


def reduce_wide(parts, wide_count):
    bits = wide_count.bit_length() - 1
    index = lax.axis_index("wide")
    states = []
    for place, part in enumerate(parts):
        order = list(range(bits))
        if place % 2 and bits > 1:
            order[0], order[1] = order[1], order[0]
        states.append((part.reshape((2,) * bits + part.shape[1:]), order, list(range(bits))[::-1]))
    for stage in range(bits):
        moved = []
        for part, order, axes in states:
            bit = order[stage]
            axis = axes.index(bit)
            mine = (index >> bit) & 1
            going = lax.dynamic_index_in_dim(part, 1 - mine, axis, keepdims=False)
            received = lax.ppermute(
                going, "wide", [(at, at ^ (1 << bit)) for at in range(wide_count)]
            )
            moved.append((axis, mine, received))
        for place, (axis, mine, received) in enumerate(moved):
            part, order, axes = states[place]
            staying = lax.dynamic_index_in_dim(part, mine, axis, keepdims=False)
            total = staying.astype(f32) + received.astype(f32)
            if stage + 1 < bits:
                total = total.astype(bf16)
            del axes[axis]
            states[place] = (total, order, axes)
    return [part for part, _, _ in states]


def rotary_rows(slots):
    half = HEAD_DIM // 2
    inverse = theta_base ** (-2.0 * jnp.arange(half, dtype=f32) / HEAD_DIM)
    angles = jnp.arange(slots, dtype=f32)[:, None] * inverse[None, :]
    cos = jnp.cos(angles)
    sin = jnp.sin(angles)
    none = jnp.zeros_like(sin)
    copies = 128 // HEAD_DIM
    return (
        jnp.tile(jnp.concatenate([cos, cos], axis=1), (1, copies)),
        jnp.tile(jnp.concatenate([-sin, none], axis=1), (1, copies)),
        jnp.tile(jnp.concatenate([none, sin], axis=1), (1, copies)),
    )


def shards(
    inputs,
    lengths,
    attn_gain,
    attn_in_weight,
    attn_out_weight,
    mlp_gain,
    mlp_in_weight,
    mlp_out_weight,
    cotangent,
):
    count = lax.axis_size("narrow")
    wide_count = lax.axis_size("wide")
    index = lax.axis_index("narrow").astype(jnp.int32)
    tokens, width = inputs.shape
    full = width * count
    seq_count = lengths.shape[0]
    slots = tokens // seq_count
    heads = width // HEAD_DIM
    hidden = mlp_in_weight.shape[2]
    half = count // 2 * width
    tables = rotary_rows(slots)
    seqs = range(seq_count)
    blocks = slots // GLUE
    meta = (index.reshape(1), lengths)

    attn_weight = lax.all_gather(
        jnp.concatenate([attn_in_weight, attn_out_weight.T[None]]), "wide", axis=1, tiled=True
    )
    mlp_weight = lax.all_gather(
        jnp.concatenate([mlp_in_weight, mlp_out_weight.T[None]]), "wide", axis=1, tiled=True
    )
    input_pieces = gather_narrow(inputs, count)
    grad_pieces = gather_narrow(cotangent, count)
    attn_gain_rows = attn_gain.reshape(count, width)
    mlp_gain_rows = mlp_gain.reshape(count, width)

    def seq_spec(seq):
        return pl.BlockSpec((slots, width), lambda step, *scalars: (seq, 0))

    row_spec = whole((slots, width))
    table_specs = [whole((slots, 128))] * 3
    gain_spec = whole((count, width))
    attn_spec = whole(attn_weight.shape)
    sizes = dict(count=count, width=width, slots=slots, full=full)

    def forward_call(seq, earlier):
        return call_kernel(
            functools.partial(attend_kernel, seq=seq, heads=heads, **sizes),
            meta,
            [*input_pieces, attn_gain_rows, attn_weight, *tables],
            [seq_spec(seq)] * count + [gain_spec, attn_spec] + table_specs,
            [((slots, full), bf16)]
            + [((slots, width), bf16)] * 4
            + [((max(heads, STAT_ROWS), slots), f32), ((STAT_ROWS, slots), f32)]
            + [((slots, half), bf16), ((slots, half), bf16)],
            [pltpu.VMEM((width, slots), bf16), pltpu.VMEM((width, BLOCK), f32)],
            24,
            earlier,
        )

    def middle_call(seq, earlier):
        return call_kernel(
            functools.partial(mlp_kernel, seq=seq, **sizes),
            meta,
            [*residual_pieces[seq], *grad_pieces, mlp_gain_rows, mlp_weight],
            [striped(width, rows=BLOCK)] * count
            + [striped(width, seq, slots // BLOCK, rows=BLOCK)] * count
            + [gain_spec, whole(mlp_weight.shape)],
            [((slots, full), bf16), ((slots, full), bf16), ((slots, hidden), bf16)]
            + [((2, slots, hidden), bf16), ((STAT_ROWS, slots), f32)]
            + [((slots, half), bf16)] * 3
            + [((slots + TAIL, half), bf16)],
            [pltpu.VMEM((STAT_ROWS, slots), f32)],
            20,
            earlier,
            slots // BLOCK,
            [striped(full, rows=BLOCK)] * 2
            + [striped(hidden, rows=BLOCK)]
            + [pl.BlockSpec((2, BLOCK, hidden), lambda step, *scalars: (0, step, 0))]
            + [pl.BlockSpec((STAT_ROWS, BLOCK), lambda step, *scalars: (0, step))]
            + [striped(half, rows=BLOCK)] * 3
            + [whole((slots + TAIL, half))],
        )

    def backward_call(seq, earlier):
        normed, queries, keys, values, attended, log_sum = forward[seq][:6]
        return call_kernel(
            functools.partial(attend_back_kernel, seq=seq, heads=heads, **sizes),
            meta,
            [*attn_grad_pieces[seq], queries, keys, values, attended, log_sum, normed]
            + [attn_gain_rows, attn_weight, *tables],
            [row_spec] * (count + 4)
            + [whole(log_sum.shape), whole((slots, full)), gain_spec, attn_spec]
            + table_specs,
            [((slots, full), bf16), ((3, slots, width), bf16), ((STAT_ROWS, slots), f32)]
            + [((slots, half), bf16), ((slots + TAIL, half), bf16)],
            [
                pltpu.VMEM((slots, width), bf16),
                pltpu.VMEM((max(heads, STAT_ROWS), slots), f32),
                pltpu.VMEM((width, slots), bf16),
                pltpu.VMEM((slots, heads * BLOCK), bf16),
                pltpu.VMEM((slots, heads * BLOCK), bf16),
                pltpu.VMEM((width, BLOCK), f32),
                pltpu.VMEM((slots, width), f32),
                pltpu.VMEM((slots, width), f32),
            ],
            26,
            earlier,
        )

    def norm_back_call(seq, parts, source, base, gains, target=None):
        terms, sums, stats = parts
        masked = target is None
        target = target or []
        outs = [((slots, width), f32), ((slots, width), bf16)]
        out_specs = [striped(width)] * 2
        if not masked:
            outs = [((tokens, width), f32)]
            out_specs = [striped(width, seq, blocks)]
        return glue_call(
            functools.partial(
                norm_back_kernel, seq=seq, terms=len(terms), slots=slots, full=full, masked=masked
            ),
            meta,
            [*terms, terms[-1], sums, stats, source[0], base[0], gains, *target],
            [striped(width)] * len(terms)
            + [tail_spec(width, slots)]
            + [whole(sums.shape), whole(stats.shape), source[1], base[1], gain_spec]
            + [pl.BlockSpec(memory_space=pl.ANY)] * len(target),
            [*outs, ((STAT_ROWS, width), f32)],
            [*out_specs, whole((STAT_ROWS, width))],
            blocks,
            [(8 + len(terms), 0)] * len(target),
        )

    forward, residuals, residual_pieces = [], [], []
    earlier = [grad_pieces[count // 2]]
    for seq in seqs:
        forward.append(forward_call(seq, earlier))
        earlier = [forward[seq][6]]
    for seq in seqs:
        terms, _ = reduce_narrow(forward[seq][7], forward[seq][8], None, count, width)
        residual, low = glue_call(
            residual_kernel,
            (),
            [inputs, *terms],
            [striped(width, seq, blocks)] + [striped(width)] * len(terms),
            [((slots, width), f32), ((slots, width), bf16)],
            [striped(width)] * 2,
            blocks,
        )
        residuals.append(residual)
        residual_pieces.append(gather_narrow(low, count))

    middle, grad_residuals, attn_grad_pieces = [], [], []
    mlp_gain_local = 0.0
    for seq in seqs:
        middle.append(middle_call(seq, earlier))
        earlier = [middle[seq][4]]
    for seq in seqs:
        terms, sums = reduce_narrow(middle[seq][7], middle[seq][8], middle[seq][4], count, width)
        grad_residual, low, gain_part = norm_back_call(
            seq,
            (terms, sums, middle[seq][4]),
            (residuals[seq], striped(width)),
            (cotangent, striped(width, seq, blocks)),
            mlp_gain_rows,
        )
        grad_residuals.append(grad_residual)
        mlp_gain_local = mlp_gain_local + gain_part[0]
        attn_grad_pieces.append(gather_narrow(low, count))
    mlp_grads = weight_grads(
        [
            ([middle[seq][0] for seq in seqs], [middle[seq][3] for seq in seqs]),
            ([middle[seq][1] for seq in seqs], [middle[seq][2][None] for seq in seqs]),
        ],
        wide_count,
        full,
        17,
        earlier,
    )
    mlp_shard = lax.psum_scatter(
        mlp_grads.reshape(-1, hidden), "wide", scatter_dimension=0, tiled=True
    )

    backward, output, inputs_grad = [], [], []
    earlier = [mlp_grads]
    for seq in seqs:
        backward.append(backward_call(seq, earlier))
        earlier = [backward[seq][2]]
    for seq in seqs:
        terms, _ = reduce_narrow(middle[seq][5], middle[seq][6], None, count, width)
        output = glue_call(
            functools.partial(output_kernel, seq=seq, terms=len(terms)),
            meta,
            [residuals[seq], *terms, *output],
            [striped(width)] * (1 + len(terms)) + [pl.BlockSpec(memory_space=pl.ANY)] * len(output),
            [((tokens, width), f32)],
            [striped(width, seq, blocks)],
            blocks,
            [(3 + len(terms), 0)] * len(output),
        )
    attn_grads = weight_grads(
        [
            ([forward[seq][0] for seq in seqs], [backward[seq][1] for seq in seqs]),
            ([backward[seq][0] for seq in seqs], [forward[seq][4][None] for seq in seqs]),
        ],
        wide_count,
        full,
        10,
        earlier,
    )
    mlp_shard = mlp_shard.reshape(mlp_grads.shape[1:])
    kinds, rows = attn_grads.shape[1:3]
    attn_shard = jnp.concatenate(
        reduce_wide(
            [
                attn_grads[:, start : start + kinds // 2].reshape(wide_count, -1, width)
                for start in range(0, kinds, kinds // 2)
            ],
            wide_count,
        )
    ).reshape(kinds, rows, width)

    attn_gain_local = 0.0
    for seq in seqs:
        terms, sums = reduce_narrow(
            backward[seq][3], backward[seq][4], backward[seq][2], count, width
        )
        *inputs_grad, gain_part = norm_back_call(
            seq,
            (terms, sums, forward[seq][6]),
            (inputs, striped(width, seq, blocks)),
            (grad_residuals[seq], striped(width)),
            attn_gain_rows,
            inputs_grad,
        )
        attn_gain_local = attn_gain_local + gain_part[0]
    gain_grads = jnp.sum(
        lax.all_gather(jnp.stack([attn_gain_local, mlp_gain_local]), "wide"), axis=0
    )
    return (
        output[0],
        inputs_grad[0],
        gain_grads[0],
        attn_shard[:3],
        attn_shard[3].T,
        gain_grads[1],
        mlp_shard[:2].astype(f32),
        mlp_shard[2].T.astype(f32),
    )


def solution(mesh):
    in_specs = (
        P("wide", "narrow"),
        P("wide"),
        P(),
        P(None, "wide", "narrow"),
        P("narrow", "wide"),
        P(),
        P(None, "wide", "narrow"),
        P("narrow", "wide"),
        P("wide", "narrow"),
    )
    out_specs = (
        P("wide", "narrow"),
        P("wide", "narrow"),
        P("narrow"),
        P(None, "wide", "narrow"),
        P("narrow", "wide"),
        P("narrow"),
        P(None, "wide", "narrow"),
        P("narrow", "wide"),
    )
    return jax.shard_map(shards, mesh=mesh, in_specs=in_specs, out_specs=out_specs, check_vma=False)
```

```python
import functools

import jax
import jax.numpy as jnp
from jax import lax
from jax.experimental import pallas as pl
from jax.experimental.pallas import tpu as pltpu
from jax.sharding import PartitionSpec as P


HEAD_DIM = 64
epsilon = 1e-05
theta_base = 160000.0
masked_score = -1e30
BLOCK = 256
GLUE = 512
TAIL = 16
STAT_ROWS = 8
f32 = jnp.float32
bf16 = jnp.bfloat16


def dot_nn(left, right):
    return lax.dot_general(left, right, (((1,), (0,)), ((), ())), preferred_element_type=f32)


def dot_nt(left, right):
    return lax.dot_general(left, right, (((1,), (1,)), ((), ())), preferred_element_type=f32)


def dot_tn(left, right):
    return lax.dot_general(left, right, (((0,), (0,)), ((), ())), preferred_element_type=f32)


def block_rows(index):
    return pl.ds(pl.multiple_of(index * BLOCK, BLOCK), BLOCK)


def feature_block(index, distance, width):
    return pl.ds(pl.multiple_of((index ^ distance) * width, width), width)


def stacked(ref, start, rows, chunks=None):
    part = ref[slice(None) if chunks is None else chunks, start : start + rows, :]
    return part.reshape(part.shape[0] * rows, part.shape[2])


def chunk_block(index, distance, width, rows):
    per_block = width // rows
    return pl.ds((index ^ distance) * per_block, per_block)


def norm_parts(parts, full):
    mean = sum(jnp.sum(part, axis=-1, keepdims=True) for part in parts) / full
    parts = [part - mean for part in parts]
    spread = sum(jnp.sum(part * part, axis=-1, keepdims=True) for part in parts) / full
    factor = lax.rsqrt(spread + epsilon)
    return [part * factor for part in parts], mean, factor


def columns_to_rows(columns):
    lane = lax.broadcasted_iota(jnp.int32, (BLOCK, 128), 1)
    packed = jnp.zeros((BLOCK, 128), f32)
    for place, column in enumerate(columns):
        packed = jnp.where(lane == place, column, packed)
    return packed.T[0:STAT_ROWS, :]


def turn(values, cos_ref, low_ref, high_ref, rows, sign):
    parts = []
    for start in range(0, values.shape[1], 128):
        part = values[:, start : start + 128]
        swapped = pltpu.roll(part, 96, 1) * low_ref[rows, :] + pltpu.roll(part, 32, 1) * high_ref[
            rows, :
        ]
        parts.append(part * cos_ref[rows, :] + sign * swapped)
    return jnp.concatenate(parts, axis=1)


def head_only(values, head):
    lane = lax.broadcasted_iota(jnp.int32, values.shape, 1)
    inside = (lane >= head * HEAD_DIM) & (lane < (head + 1) * HEAD_DIM)
    return jnp.where(inside, values.astype(f32), 0.0).astype(bf16)


def head_pairs(heads, one_head):
    def pair(place, carry):
        one_head(2 * place)
        one_head(2 * place + 1)
        return carry

    lax.fori_loop(0, heads // 2, pair, 0)


def send_tail(send, slots, first, second):
    lanes = send.shape[1]
    pieces = [row[:, start : start + lanes] for row in (first, second) for start in range(0, slots, lanes)]
    if len(pieces) < TAIL:
        pieces.append(jnp.zeros((TAIL - len(pieces), lanes), f32))
    send[slots : slots + TAIL, :] = jnp.concatenate(pieces, axis=0).astype(bf16)


def attend_kernel(place_ref, lengths, *refs, seq, count, width, heads, slots, full):
    pieces = refs[:count]
    gain, first_weight, second_weight, cos_ref, low_ref, high_ref = refs[count : count + 6]
    normed, q_out, k_out, v_out, attended, log_sum, stats, keep, send = refs[count + 6 : count + 15]
    values_t, out_t = refs[count + 15 :]
    chunk = first_weight.shape[1] // 2
    index = place_ref[0]
    length = lengths[seq]
    live = pl.cdiv(length, BLOCK)
    blocks = slots // BLOCK

    def project(block, carry):
        rows = block_rows(block)
        units, mean, factor = norm_parts([piece[rows, :].astype(f32) for piece in pieces], full)
        for place, unit in enumerate(units):
            gained = unit * gain[pl.ds(index ^ place, 1), :]
            normed[rows, feature_block(index, place, width)] = gained.astype(bf16)
        stats[:, rows] = columns_to_rows((mean, factor))
        row = normed[rows, :]
        turned = turn(dot_nn(row, stacked(first_weight, 0, chunk)), cos_ref, low_ref, high_ref, rows, 1.0)
        q_out[rows, :] = (turned.astype(bf16).astype(f32) * HEAD_DIM**-0.5).astype(bf16)
        turned = turn(dot_nn(row, stacked(first_weight, chunk, chunk)), cos_ref, low_ref, high_ref, rows, 1.0)
        k_out[rows, :] = turned.astype(bf16)
        v_out[rows, :] = dot_nn(row, stacked(second_weight, 0, chunk)).astype(bf16)
        return carry

    def clear(block, carry):
        rows = block_rows(block)
        normed[rows, :] = jnp.zeros((BLOCK, full), bf16)
        for ref in (q_out, k_out, v_out, attended):
            ref[rows, :] = jnp.zeros((BLOCK, width), bf16)
        stats[:, rows] = jnp.zeros((STAT_ROWS, BLOCK), f32)
        keep[rows, :] = jnp.zeros((BLOCK, keep.shape[1]), bf16)
        send[rows, :] = jnp.zeros((BLOCK, send.shape[1]), bf16)
        return carry

    lax.fori_loop(0, live, project, 0)
    lax.fori_loop(live, blocks, clear, 0)
    log_sum[...] = jnp.zeros(log_sum.shape, f32)

    def attend(count_live):
        span = count_live * BLOCK
        values_t[:, 0:span] = v_out[0:span, :].T

        def query_block(block, carry):
            rows = block_rows(block)
            queries = q_out[rows, :]

            def one_head(head):
                mine = pl.ds(pl.multiple_of(head * HEAD_DIM, HEAD_DIM), HEAD_DIM)
                scores = dot_nt(k_out[0:span, :], head_only(queries, head))
                slot = lax.broadcasted_iota(jnp.int32, (span, BLOCK), 0)
                scores = jnp.where(slot < length, scores, masked_score)
                top = jnp.max(scores, axis=0, keepdims=True)
                weights = jnp.exp(scores - top)
                total = jnp.sum(weights, axis=0, keepdims=True)
                result = dot_nn(values_t[mine, 0:span], weights.astype(bf16))
                out_t[mine, :] = result * (1.0 / total)
                log_sum[pl.ds(head, 1), rows] = top + jnp.log(total)

            head_pairs(heads, one_head)
            attended[rows, :] = out_t[...].T.astype(bf16)
            return carry

        lax.fori_loop(0, count_live, query_block, 0)

    for count_live in range(1, blocks + 1):
        pl.when(live == count_live)(functools.partial(attend, count_live))

    def output(block, carry):
        rows = block_rows(block)
        row = attended[rows, :]
        for place in range(count):
            mine = chunk_block(index, place, width, chunk)
            part = dot_nt(row, stacked(second_weight, chunk, chunk, mine))
            target = slice((place // 2) * width, (place // 2 + 1) * width)
            if place % 2:
                send[rows, target] = part.astype(bf16)
            else:
                keep[rows, target] = part.astype(bf16)
        return carry

    lax.fori_loop(0, live, output, 0)


def mlp_kernel(place_ref, lengths, *refs, seq, count, width, slots, full):
    rows_in = refs[:count]
    grads_in = refs[count : 2 * count]
    gain, first_weight, second_weight = refs[2 * count : 2 * count + 3]
    (normed, grads, mixed, grad_expanded, stats, out_keep, out_send, back_keep, back_send) = refs[
        2 * count + 3 : 2 * count + 12
    ]
    kept, down = refs[2 * count + 12 :]
    half = first_weight.shape[1] // 3
    chunk = 2 * half
    index = place_ref[0]
    length = lengths[seq]
    block = pl.program_id(0)
    rows = block_rows(block)

    @pl.when(block == 0)
    def _():
        for place in range(first_weight.shape[0]):
            start = place * chunk
            down[start : start + half, :] = first_weight[place, chunk : chunk + half, :]
            down[start + half : start + chunk, :] = second_weight[place, chunk : chunk + half, :]

    @pl.when(block * BLOCK < length)
    def _():
        slot = block * BLOCK + lax.broadcasted_iota(jnp.int32, (BLOCK, 1), 0)
        units, mean, factor = norm_parts([piece[...].astype(f32) for piece in rows_in], full)
        for place, unit in enumerate(units):
            here = feature_block(index, place, width)
            gained = unit * gain[pl.ds(index ^ place, 1), :]
            normed[:, here] = gained.astype(bf16)
            grad = jnp.where(slot < length, grads_in[place][...].astype(f32), 0.0)
            grads[:, here] = grad.astype(bf16)
        row = normed[...]
        grad = grads[...]
        gate = dot_nn(row, stacked(first_weight, 0, chunk))
        linear = dot_nn(row, stacked(second_weight, 0, chunk))
        grad_mixed = dot_nn(grad, down[...])
        phi = 0.5 + 0.5 * lax.erf(gate * (0.5**0.5))
        activated = gate * phi
        density = jnp.exp(-0.5 * gate * gate) * (0.5 / jnp.pi) ** 0.5
        mixed_low = (activated * linear).astype(bf16)
        mixed[...] = mixed_low
        first = (grad_mixed * linear * (phi + gate * density)).astype(bf16)
        second = (grad_mixed * activated).astype(bf16)
        grad_expanded[0] = first
        grad_expanded[1] = second
        plain_sum = jnp.zeros((BLOCK, 1), f32)
        unit_sum = jnp.zeros((BLOCK, 1), f32)
        for place in range(count):
            here = feature_block(index, place, width)
            target = slice((place // 2) * width, (place // 2 + 1) * width)
            mine = chunk_block(index, place, width, chunk)
            part = dot_nt(mixed_low, down[here, :])
            back = dot_nt(first, stacked(first_weight, 0, chunk, mine))
            back += dot_nt(second, stacked(second_weight, 0, chunk, mine))
            plain_sum += jnp.sum(back * gain[pl.ds(index ^ place, 1), :], axis=-1, keepdims=True)
            unit_sum += jnp.sum(back * normed[:, here].astype(f32), axis=-1, keepdims=True)
            if place % 2:
                out_send[:, target] = part.astype(bf16)
                back_send[rows, target] = back.astype(bf16)
            else:
                out_keep[:, target] = part.astype(bf16)
                back_keep[:, target] = back.astype(bf16)
        lines = columns_to_rows((mean, factor, plain_sum, unit_sum))
        stats[...] = lines
        kept[:, rows] = lines

    @pl.when(block * BLOCK >= length)
    def _():
        for ref in (normed, grads, mixed, out_keep, out_send, back_keep, grad_expanded, stats):
            ref[...] = jnp.zeros(ref.shape, ref.dtype)
        back_send[rows, :] = jnp.zeros((BLOCK, back_send.shape[1]), bf16)
        kept[:, rows] = jnp.zeros((STAT_ROWS, BLOCK), f32)

    @pl.when(block == pl.num_programs(0) - 1)
    def _():
        send_tail(back_send, slots, kept[2:3, :], kept[3:4, :])


def attend_back_kernel(place_ref, lengths, *refs, seq, count, width, heads, slots, full):
    grads_in = refs[:count]
    q_in, k_in, v_in, attended, log_sum, normed, gain = refs[count : count + 7]
    first_weight, second_weight, cos_ref, low_ref, high_ref = refs[count + 7 : count + 12]
    grads, grad_projected, stats, keep, send = refs[count + 12 : count + 17]
    (grad_att, delta, keys_t, probs_all, scores_all, query_t, key_total, value_total) = refs[
        count + 17 : count + 25
    ]
    queries_all, grads_all = refs[count + 25 :]
    chunk = first_weight.shape[1] // 2
    places = ((first_weight, 0), (first_weight, chunk), (second_weight, 0))
    index = place_ref[0]
    length = lengths[seq]
    live = pl.cdiv(length, BLOCK)
    blocks = slots // BLOCK

    def enter(block, carry):
        rows = block_rows(block)
        for place in range(count):
            grads[rows, feature_block(index, place, width)] = grads_in[place][rows, :]
        grad = dot_nn(grads[rows, :], stacked(second_weight, chunk, chunk)).astype(bf16)
        grad_att[rows, :] = grad
        inner = (grad.astype(f32) * attended[rows, :].astype(f32)).T
        for head in range(heads):
            mine = slice(head * HEAD_DIM, (head + 1) * HEAD_DIM)
            delta[head : head + 1, rows] = jnp.sum(inner[mine, :], axis=0, keepdims=True)
        return carry

    def clear(block, carry):
        rows = block_rows(block)
        grads[rows, :] = jnp.zeros((BLOCK, full), bf16)
        for place in range(3):
            grad_projected[place, rows, :] = jnp.zeros((BLOCK, width), bf16)
        stats[:, rows] = jnp.zeros((STAT_ROWS, BLOCK), f32)
        keep[rows, :] = jnp.zeros((BLOCK, keep.shape[1]), bf16)
        send[rows, :] = jnp.zeros((BLOCK, send.shape[1]), bf16)
        return carry

    lax.fori_loop(0, live, enter, 0)
    lax.fori_loop(live, blocks, clear, 0)

    def attend(count_live):
        span = count_live * BLOCK
        keys_t[:, 0:span] = k_in[0:span, :].T
        key_total[0:span, :] = jnp.zeros((span, width), f32)
        value_total[0:span, :] = jnp.zeros((span, width), f32)

        def query_block(block, carry):
            rows = block_rows(block)

            def one_head(head):
                mine = pl.ds(pl.multiple_of(head * HEAD_DIM, HEAD_DIM), HEAD_DIM)
                lanes = pl.ds(pl.multiple_of(head * BLOCK, BLOCK), BLOCK)
                queries = head_only(q_in[rows, :], head)
                grad_rows = head_only(grad_att[rows, :], head)
                queries_all[lanes, :] = queries
                grads_all[lanes, :] = grad_rows
                scores = dot_nt(k_in[0:span, :], queries)
                slot = lax.broadcasted_iota(jnp.int32, (span, BLOCK), 0)
                scores = jnp.where(slot < length, scores, masked_score)
                weights = jnp.exp(scores - log_sum[pl.ds(head, 1), rows])
                grad_weights = dot_nt(v_in[0:span, :], grad_rows)
                grad_scores = (weights * (grad_weights - delta[pl.ds(head, 1), rows])).astype(bf16)
                probs_all[0:span, lanes] = weights.astype(bf16)
                scores_all[0:span, lanes] = grad_scores
                query_t[mine, :] = dot_nn(keys_t[mine, 0:span], grad_scores)

            head_pairs(heads, one_head)
            value_total[0:span, :] += dot_nn(probs_all[0:span, :], grads_all[...])
            key_total[0:span, :] += dot_nn(scores_all[0:span, :], queries_all[...])
            turned = turn(query_t[...].T * HEAD_DIM**-0.5, cos_ref, low_ref, high_ref, rows, -1.0)
            grad_projected[0, rows, :] = turned.astype(bf16)
            return carry

        lax.fori_loop(0, count_live, query_block, 0)

    for count_live in range(1, blocks + 1):
        pl.when(live == count_live)(functools.partial(attend, count_live))

    def leave(block, carry):
        rows = block_rows(block)
        turned = turn(key_total[rows, :], cos_ref, low_ref, high_ref, rows, -1.0)
        grad_projected[1, rows, :] = turned.astype(bf16)
        grad_projected[2, rows, :] = value_total[rows, :].astype(bf16)
        plain_sum = jnp.zeros((BLOCK, 1), f32)
        unit_sum = jnp.zeros((BLOCK, 1), f32)
        for place in range(count):
            here = feature_block(index, place, width)
            mine = chunk_block(index, place, width, chunk)
            target = slice((place // 2) * width, (place // 2 + 1) * width)
            back = sum(
                dot_nt(grad_projected[kind, rows, :], stacked(ref, start, chunk, mine))
                for kind, (ref, start) in enumerate(places)
            )
            plain_sum += jnp.sum(back * gain[pl.ds(index ^ place, 1), :], axis=-1, keepdims=True)
            unit_sum += jnp.sum(back * normed[rows, here].astype(f32), axis=-1, keepdims=True)
            if place % 2:
                send[rows, target] = back.astype(bf16)
            else:
                keep[rows, target] = back.astype(bf16)
        zero = jnp.zeros((BLOCK, 1), f32)
        stats[:, rows] = columns_to_rows((zero, zero, plain_sum, unit_sum))
        return carry

    lax.fori_loop(0, live, leave, 0)
    send_tail(send, slots, stats[2:3, :], stats[3:4, :])


def rows_to_columns(rows):
    filler = jnp.zeros((128 - len(rows), rows[0].shape[1]), f32)
    return jnp.concatenate([*rows, filler], axis=0).T


def read_tail(tail, slots):
    values = tail[...].astype(f32)
    lanes = values.shape[1]
    lines = slots // lanes
    return [
        jnp.concatenate([values[row : row + 1] for row in range(start, start + lines)], axis=1)
        for start in (0, lines)
    ]


def near_kernel(*refs, blocks, terms, width, slots, tailed):
    parts = refs[: blocks * terms]
    going = refs[blocks * terms + 2 * tailed]
    step = pl.program_id(0)
    here = pl.ds(pl.multiple_of(step * GLUE, GLUE), GLUE)
    for block in range(blocks):
        total = sum(ref[...].astype(f32) for ref in parts[block * terms : (block + 1) * terms])
        going[here, block * width : (block + 1) * width] = total.astype(bf16)
    if tailed:
        tail, sums = refs[blocks * terms : blocks * terms + 2]
        sums_out = refs[-1]

        @pl.when(step == 0)
        def _():
            plain, unit = read_tail(tail, slots)
            plain = plain + sums[2:3, :]
            unit = unit + sums[3:4, :]
            empty = jnp.zeros((2, slots), f32)
            sums_out[...] = jnp.concatenate([empty, plain, unit, empty, empty], axis=0)
            send_tail(going, slots, plain, unit)


def residual_kernel(inputs, *refs):
    *terms, out, low = refs
    total = inputs[...].astype(f32) + sum(term[...].astype(f32) for term in terms)
    out[...] = total
    low[...] = total.astype(bf16)


def output_kernel(place_ref, lengths, residual, *refs, seq, terms):
    out = refs[-1]
    slot = pl.program_id(0) * GLUE + lax.broadcasted_iota(jnp.int32, (GLUE, 1), 0)
    total = residual[...] + sum(term[...].astype(f32) for term in refs[:terms])
    out[...] = jnp.where(slot < lengths[seq], total, 0.0)


def norm_back_kernel(place_ref, lengths, *refs, seq, terms, slots, full, masked):
    parts = refs[:terms]
    (tail, sums, stats, source, base, gain) = refs[terms : terms + 6]
    low = refs[-2] if masked else None
    out = refs[-3] if masked else refs[-2]
    gain_grad = refs[-1]
    step = pl.program_id(0)
    plain, unit_sum = read_tail(tail, slots)
    here = pl.ds(pl.multiple_of(step * GLUE, GLUE), GLUE)
    columns = rows_to_columns([stats[0:1, here], stats[1:2, here], sums[2:3, here], sums[3:4, here]])
    lane_block = [plain[:, start : start + GLUE] for start in range(0, slots, GLUE)]
    unit_block = [unit_sum[:, start : start + GLUE] for start in range(0, slots, GLUE)]
    more_plain = lane_block[0]
    more_unit = unit_block[0]
    for place in range(1, len(lane_block)):
        more_plain = jnp.where(step == place, lane_block[place], more_plain)
        more_unit = jnp.where(step == place, unit_block[place], more_unit)
    more = rows_to_columns([more_plain, more_unit])
    mean, factor = columns[:, 0:1], columns[:, 1:2]
    plain_mean = (columns[:, 2:3] + more[:, 0:1]) / full
    unit_mean = (columns[:, 3:4] + more[:, 1:2]) / full
    unit = (source[...].astype(f32) - mean) * factor
    gradient = sum(part[...].astype(f32) for part in parts)
    inner = gradient * gain[pl.ds(place_ref[0], 1), :] - plain_mean - unit * unit_mean
    below = base[...].astype(f32)
    if masked:
        slot = step * GLUE + lax.broadcasted_iota(jnp.int32, (GLUE, 1), 0)
        below = jnp.where(slot < lengths[seq], below, 0.0)
    total = below + factor * inner
    out[...] = total
    if masked:
        low[...] = total.astype(bf16)

    @pl.when(step == 0)
    def _():
        gain_grad[...] = jnp.zeros(gain_grad.shape, f32)

    gain_grad[0:1, :] += jnp.sum(gradient * unit, axis=0, keepdims=True)


def grad_kernel(*refs, pairs, seq_count, layout):
    outs = refs[-2:]
    cursor = 0
    pieces = iter(layout)
    for kinds in pairs:
        lefts = refs[cursor : cursor + seq_count]
        rights = refs[cursor + seq_count : cursor + 2 * seq_count]
        cursor += 2 * seq_count
        for kind in range(kinds):
            total = sum(dot_tn(left[...], right[kind]) for left, right in zip(lefts, rights))
            moves = next(pieces)
            rows = sum(size for _, _, size in moves)
            for step in range(outs[0].shape[0]):
                start = step * rows
                for out, target, size in moves:
                    part = total[start : start + size, :].astype(bf16)
                    outs[out][step, target : target + size, :] = part
                    start += size


def weight_grads(groups, layout, wide_count, full, micros, earlier):
    rows = full // wide_count
    per_step = max(BLOCK // rows, 1)
    columns = groups[0][1][0].shape[2]
    slots = groups[0][0][0].shape[0]
    seq_count = len(groups[0][0])
    pairs = tuple(rights[0].shape[0] for _, rights in groups)
    operands = []
    specs = []
    for lefts, rights in groups:
        for left in lefts:
            operands.append(left)
            specs.append(pl.BlockSpec((slots, rows * per_step), lambda step: (0, step)))
        for right in rights:
            operands.append(right)
            specs.append(pl.BlockSpec(right.shape, lambda step: (0, 0, 0)))
    lines = sum(pairs) * rows // 2
    body = functools.partial(grad_kernel, pairs=pairs, seq_count=seq_count, layout=layout)
    body, operands, specs = after(body, operands, specs, earlier, 0)
    return pl.pallas_call(
        body,
        grid=(wide_count // per_step,),
        in_specs=specs,
        out_specs=[pl.BlockSpec((per_step, lines, columns), lambda step: (step, 0, 0))] * 2,
        out_shape=[jax.ShapeDtypeStruct((wide_count, lines, columns), bf16)] * 2,
        cost_estimate=estimate(micros),
    )(*operands)


def whole(shape):
    return pl.BlockSpec(shape, lambda step, *scalars: (0,) * len(shape))


def striped(columns, seq=0, blocks=0, column=0, rows=GLUE):
    return pl.BlockSpec((rows, columns), lambda step, *scalars: (seq * blocks + step, column))


def tail_spec(columns, slots):
    return pl.BlockSpec((TAIL, columns), lambda step, *scalars: (slots // TAIL, 0))


def after(body, operands, specs, earlier, scalars):
    place = scalars + len(operands)

    def ordered(*refs):
        return body(*refs[:place], *refs[place + len(earlier) :])

    unread = [pl.BlockSpec(memory_space=pl.ANY)] * len(earlier)
    return ordered, [*operands, *earlier], [*specs, *unread]


def estimate(micros):
    return pl.CostEstimate(flops=int(micros * 1e9), transcendentals=0, bytes_accessed=1 << 20)


def glue_call(body, scalars, operands, specs, outs, out_specs, steps, aliases=()):
    return pl.pallas_call(
        body,
        grid_spec=pltpu.PrefetchScalarGridSpec(
            num_scalar_prefetch=len(scalars), grid=(steps,), in_specs=specs, out_specs=out_specs
        ),
        out_shape=[jax.ShapeDtypeStruct(shape, kind) for shape, kind in outs],
        input_output_aliases=dict(aliases),
        cost_estimate=estimate(2),
    )(*scalars, *operands)


def call_kernel(
    body, meta, operands, specs, outs, scratch, micros, earlier, steps=1, out_specs=None
):
    body, operands, specs = after(body, operands, specs, earlier, 2)
    return pl.pallas_call(
        body,
        grid_spec=pltpu.PrefetchScalarGridSpec(
            num_scalar_prefetch=2,
            grid=(steps,),
            in_specs=specs,
            out_specs=out_specs or [whole(shape) for shape, _ in outs],
            scratch_shapes=scratch,
        ),
        out_shape=[jax.ShapeDtypeStruct(shape, kind) for shape, kind in outs],
        cost_estimate=estimate(micros),
    )(*meta, *operands)


def swap(values, distance, count):
    return lax.ppermute(values, "narrow", [(place, place ^ distance) for place in range(count)])


def gather_narrow(own, count):
    pieces = {0: own}
    distance = count // 2
    while distance:
        for place in sorted(pieces):
            pieces[place | distance] = swap(pieces[place], distance, count)
        distance //= 2
    return [pieces[place] for place in range(count)]


def reduce_narrow(keep, send, sums, count, width):
    slots = keep.shape[0]
    tailed = sums is not None
    received = swap(send, 1, count)
    terms = [(keep, 1), (received, 1)]
    blocks = count // 2
    distance = 2
    while distance < count:
        blocks //= 2
        operands = []
        specs = []
        for block in range(blocks):
            for term, stride in terms:
                operands.append(term)
                specs.append(striped(width, column=(2 * block + 1) * stride))
        lanes = blocks * width
        outs = [((slots + TAIL * tailed, lanes), bf16)]
        if tailed:
            operands += [received, sums]
            specs += [tail_spec(received.shape[1], slots), whole(sums.shape)]
            outs.append((sums.shape, f32))
        body = functools.partial(
            near_kernel, blocks=blocks, terms=len(terms), width=width, slots=slots, tailed=tailed
        )
        going, *rest = glue_call(
            body, (), operands, specs, outs, [whole(shape) for shape, _ in outs], slots // GLUE
        )
        if tailed:
            sums = rest[0]
        received = swap(going, distance, count)
        terms = [(term, 2 * stride) for term, stride in terms] + [(received, 1)]
        distance *= 2
    return [term for term, _ in terms], sums


def swap_wide(values, bit, wide_count):
    return lax.ppermute(values, "wide", [(at, at ^ (1 << bit)) for at in range(wide_count)])


def bit_orders(wide_count):
    bits = wide_count.bit_length() - 1
    first = list(range(bits))
    return first, first[1::-1] + first[2:]


def gather_wide(parts, wide_count):
    bits = wide_count.bit_length() - 1
    index = lax.axis_index("wide")
    mine = [(index >> bit) & 1 for bit in range(bits)]
    zero = jnp.zeros((), mine[0].dtype)
    whole_parts = []
    for part in parts:
        space = jnp.zeros((2,) * bits + part.shape, part.dtype)
        start = mine[::-1] + [zero, zero]
        whole_parts.append(lax.dynamic_update_slice(space, part.reshape((1,) * bits + part.shape), start))
    for stage in range(bits):
        moved = []
        for place, order in enumerate(bit_orders(wide_count)):
            done = order[::-1][:stage]
            start = [zero if bit in done else mine[bit] for bit in range(bits)][::-1]
            sizes = [2 if bit in done else 1 for bit in range(bits)][::-1]
            going = lax.dynamic_slice(
                whole_parts[place], start + [zero, zero], sizes + list(parts[place].shape)
            )
            bit = order[::-1][stage]
            received = swap_wide(going, bit, wide_count)
            start[bits - 1 - bit] = 1 - mine[bit]
            moved.append((received, start))
        for place, (received, start) in enumerate(moved):
            whole_parts[place] = lax.dynamic_update_slice(
                whole_parts[place], received, start + [zero, zero]
            )
    return [
        space.reshape((wide_count,) + part.shape) for space, part in zip(whole_parts, parts)
    ]


def sum_wide(values, wide_count):
    for bit in range(wide_count.bit_length() - 1):
        values = values + swap_wide(values, bit, wide_count)
    return values


def reduce_wide(parts, wide_count):
    bits = wide_count.bit_length() - 1
    index = lax.axis_index("wide")
    states = []
    for part, order in zip(parts, bit_orders(wide_count)):
        states.append((part.reshape((2,) * bits + part.shape[1:]), order, list(range(bits))[::-1]))
    for stage in range(bits):
        moved = []
        for part, order, axes in states:
            bit = order[stage]
            axis = axes.index(bit)
            mine = (index >> bit) & 1
            going = lax.dynamic_index_in_dim(part, 1 - mine, axis, keepdims=False)
            received = swap_wide(going, bit, wide_count)
            moved.append((axis, mine, received))
        for place, (axis, mine, received) in enumerate(moved):
            part, order, axes = states[place]
            staying = lax.dynamic_index_in_dim(part, mine, axis, keepdims=False)
            total = staying.astype(f32) + received.astype(f32)
            if stage + 1 < bits:
                total = total.astype(bf16)
            del axes[axis]
            states[place] = (total, order, axes)
    return [part for part, _, _ in states]


def rotary_rows(slots):
    half = HEAD_DIM // 2
    inverse = theta_base ** (-2.0 * jnp.arange(half, dtype=f32) / HEAD_DIM)
    angles = jnp.arange(slots, dtype=f32)[:, None] * inverse[None, :]
    cos = jnp.cos(angles)
    sin = jnp.sin(angles)
    none = jnp.zeros_like(sin)
    copies = 128 // HEAD_DIM
    return (
        jnp.tile(jnp.concatenate([cos, cos], axis=1), (1, copies)),
        jnp.tile(jnp.concatenate([-sin, none], axis=1), (1, copies)),
        jnp.tile(jnp.concatenate([none, sin], axis=1), (1, copies)),
    )


def shards(
    inputs,
    lengths,
    attn_gain,
    attn_in_weight,
    attn_out_weight,
    mlp_gain,
    mlp_in_weight,
    mlp_out_weight,
    cotangent,
):
    count = lax.axis_size("narrow")
    wide_count = lax.axis_size("wide")
    index = lax.axis_index("narrow").astype(jnp.int32)
    tokens, width = inputs.shape
    full = width * count
    seq_count = lengths.shape[0]
    slots = tokens // seq_count
    heads = width // HEAD_DIM
    hidden = mlp_in_weight.shape[2]
    half = count // 2 * width
    tables = rotary_rows(slots)
    seqs = range(seq_count)
    blocks = slots // GLUE
    meta = (index.reshape(1), lengths)

    rows = full // wide_count
    out_turned = attn_out_weight.T
    attn_weights = gather_wide(
        [
            attn_in_weight[:2].reshape(2 * rows, width),
            jnp.concatenate([attn_in_weight[2], out_turned]),
        ],
        wide_count,
    )
    down_turned = mlp_out_weight.T
    mlp_weights = gather_wide(
        [
            jnp.concatenate([mlp_in_weight[0], down_turned[: rows // 2]]),
            jnp.concatenate([mlp_in_weight[1], down_turned[rows // 2 :]]),
        ],
        wide_count,
    )
    input_pieces = gather_narrow(inputs, count)
    grad_pieces = gather_narrow(cotangent, count)
    attn_gain_rows = attn_gain.reshape(count, width)
    mlp_gain_rows = mlp_gain.reshape(count, width)

    def seq_spec(seq):
        return pl.BlockSpec((slots, width), lambda step, *scalars: (seq, 0))

    row_spec = whole((slots, width))
    table_specs = [whole((slots, 128))] * 3
    gain_spec = whole((count, width))
    attn_specs = [whole(part.shape) for part in attn_weights]
    mlp_specs = [whole(part.shape) for part in mlp_weights]
    sizes = dict(count=count, width=width, slots=slots, full=full)

    def forward_call(seq, earlier):
        return call_kernel(
            functools.partial(attend_kernel, seq=seq, heads=heads, **sizes),
            meta,
            [*input_pieces, attn_gain_rows, *attn_weights, *tables],
            [seq_spec(seq)] * count + [gain_spec] + attn_specs + table_specs,
            [((slots, full), bf16)]
            + [((slots, width), bf16)] * 4
            + [((max(heads, STAT_ROWS), slots), f32), ((STAT_ROWS, slots), f32)]
            + [((slots, half), bf16), ((slots, half), bf16)],
            [pltpu.VMEM((width, slots), bf16), pltpu.VMEM((width, BLOCK), f32)],
            24,
            earlier,
        )

    def middle_call(seq, earlier):
        return call_kernel(
            functools.partial(mlp_kernel, seq=seq, **sizes),
            meta,
            [*residual_pieces[seq], *grad_pieces, mlp_gain_rows, *mlp_weights],
            [striped(width, rows=BLOCK)] * count
            + [striped(width, seq, slots // BLOCK, rows=BLOCK)] * count
            + [gain_spec]
            + mlp_specs,
            [((slots, full), bf16), ((slots, full), bf16), ((slots, hidden), bf16)]
            + [((2, slots, hidden), bf16), ((STAT_ROWS, slots), f32)]
            + [((slots, half), bf16)] * 3
            + [((slots + TAIL, half), bf16)],
            [pltpu.VMEM((STAT_ROWS, slots), f32), pltpu.VMEM((full, hidden), bf16)],
            20,
            earlier,
            slots // BLOCK,
            [striped(full, rows=BLOCK)] * 2
            + [striped(hidden, rows=BLOCK)]
            + [pl.BlockSpec((2, BLOCK, hidden), lambda step, *scalars: (0, step, 0))]
            + [pl.BlockSpec((STAT_ROWS, BLOCK), lambda step, *scalars: (0, step))]
            + [striped(half, rows=BLOCK)] * 3
            + [whole((slots + TAIL, half))],
        )

    def backward_call(seq, earlier):
        normed, queries, keys, values, attended, log_sum = forward[seq][:6]
        return call_kernel(
            functools.partial(attend_back_kernel, seq=seq, heads=heads, **sizes),
            meta,
            [*attn_grad_pieces[seq], queries, keys, values, attended, log_sum, normed]
            + [attn_gain_rows, *attn_weights, *tables],
            [row_spec] * (count + 4)
            + [whole(log_sum.shape), whole((slots, full)), gain_spec]
            + attn_specs
            + table_specs,
            [((slots, full), bf16), ((3, slots, width), bf16), ((STAT_ROWS, slots), f32)]
            + [((slots, half), bf16), ((slots + TAIL, half), bf16)],
            [
                pltpu.VMEM((slots, width), bf16),
                pltpu.VMEM((max(heads, STAT_ROWS), slots), f32),
                pltpu.VMEM((width, slots), bf16),
                pltpu.VMEM((slots, heads * BLOCK), bf16),
                pltpu.VMEM((slots, heads * BLOCK), bf16),
                pltpu.VMEM((width, BLOCK), f32),
                pltpu.VMEM((slots, width), f32),
                pltpu.VMEM((slots, width), f32),
                pltpu.VMEM((heads * BLOCK, width), bf16),
                pltpu.VMEM((heads * BLOCK, width), bf16),
            ],
            26,
            earlier,
        )

    def norm_back_call(seq, parts, source, base, gains, target=None):
        terms, sums, stats = parts
        masked = target is None
        target = target or []
        outs = [((slots, width), f32), ((slots, width), bf16)]
        out_specs = [striped(width)] * 2
        if not masked:
            outs = [((tokens, width), f32)]
            out_specs = [striped(width, seq, blocks)]
        return glue_call(
            functools.partial(
                norm_back_kernel, seq=seq, terms=len(terms), slots=slots, full=full, masked=masked
            ),
            meta,
            [*terms, terms[-1], sums, stats, source[0], base[0], gains, *target],
            [striped(width)] * len(terms)
            + [tail_spec(width, slots)]
            + [whole(sums.shape), whole(stats.shape), source[1], base[1], gain_spec]
            + [pl.BlockSpec(memory_space=pl.ANY)] * len(target),
            [*outs, ((STAT_ROWS, width), f32)],
            [*out_specs, whole((STAT_ROWS, width))],
            blocks,
            [(8 + len(terms), 0)] * len(target),
        )

    forward, residuals, residual_pieces = [], [], []
    earlier = [grad_pieces[count // 2]]
    for seq in seqs:
        forward.append(forward_call(seq, earlier))
        earlier = [forward[seq][6]]
    for seq in seqs:
        terms, _ = reduce_narrow(forward[seq][7], forward[seq][8], None, count, width)
        residual, low = glue_call(
            residual_kernel,
            (),
            [inputs, *terms],
            [striped(width, seq, blocks)] + [striped(width)] * len(terms),
            [((slots, width), f32), ((slots, width), bf16)],
            [striped(width)] * 2,
            blocks,
        )
        residuals.append(residual)
        residual_pieces.append(gather_narrow(low, count))

    middle, grad_residuals, attn_grad_pieces = [], [], []
    mlp_gain_local = 0.0
    for seq in seqs:
        middle.append(middle_call(seq, earlier))
        earlier = [middle[seq][4]]
    for seq in seqs:
        terms, sums = reduce_narrow(middle[seq][7], middle[seq][8], middle[seq][4], count, width)
        grad_residual, low, gain_part = norm_back_call(
            seq,
            (terms, sums, middle[seq][4]),
            (residuals[seq], striped(width)),
            (cotangent, striped(width, seq, blocks)),
            mlp_gain_rows,
        )
        grad_residuals.append(grad_residual)
        mlp_gain_local = mlp_gain_local + gain_part[0]
        attn_grad_pieces.append(gather_narrow(low, count))
    mlp_grads = weight_grads(
        [
            ([middle[seq][0] for seq in seqs], [middle[seq][3] for seq in seqs]),
            ([middle[seq][1] for seq in seqs], [middle[seq][2][None] for seq in seqs]),
        ],
        (((0, 0, rows),), ((1, 0, rows),), ((0, rows, rows // 2), (1, rows, rows // 2))),
        wide_count,
        full,
        17,
        earlier,
    )
    mlp_first, mlp_second = reduce_wide(mlp_grads, wide_count)

    backward, output, inputs_grad = [], [], []
    earlier = [mlp_grads[0]]
    for seq in seqs:
        backward.append(backward_call(seq, earlier))
        earlier = [backward[seq][2]]
    for seq in seqs:
        terms, _ = reduce_narrow(middle[seq][5], middle[seq][6], None, count, width)
        output = glue_call(
            functools.partial(output_kernel, seq=seq, terms=len(terms)),
            meta,
            [residuals[seq], *terms, *output],
            [striped(width)] * (1 + len(terms)) + [pl.BlockSpec(memory_space=pl.ANY)] * len(output),
            [((tokens, width), f32)],
            [striped(width, seq, blocks)],
            blocks,
            [(3 + len(terms), 0)] * len(output),
        )
    attn_grads = weight_grads(
        [
            ([forward[seq][0] for seq in seqs], [backward[seq][1] for seq in seqs]),
            ([backward[seq][0] for seq in seqs], [forward[seq][4][None] for seq in seqs]),
        ],
        (((0, 0, rows),), ((0, rows, rows),), ((1, 0, rows),), ((1, rows, rows),)),
        wide_count,
        full,
        10,
        earlier,
    )
    attn_first, attn_second = reduce_wide(attn_grads, wide_count)

    attn_gain_local = 0.0
    for seq in seqs:
        terms, sums = reduce_narrow(
            backward[seq][3], backward[seq][4], backward[seq][2], count, width
        )
        *inputs_grad, gain_part = norm_back_call(
            seq,
            (terms, sums, forward[seq][6]),
            (inputs, striped(width, seq, blocks)),
            (grad_residuals[seq], striped(width)),
            attn_gain_rows,
            inputs_grad,
        )
        attn_gain_local = attn_gain_local + gain_part[0]
    gain_grads = sum_wide(jnp.stack([attn_gain_local, mlp_gain_local]), wide_count)
    return (
        output[0],
        inputs_grad[0],
        gain_grads[0],
        jnp.stack([attn_first[:rows], attn_first[rows:], attn_second[:rows]]),
        attn_second[rows:].T,
        gain_grads[1],
        jnp.stack([mlp_first[:rows], mlp_second[:rows]]),
        jnp.concatenate([mlp_first[rows:], mlp_second[rows:]]).T,
    )


def solution(mesh):
    in_specs = (
        P("wide", "narrow"),
        P("wide"),
        P(),
        P(None, "wide", "narrow"),
        P("narrow", "wide"),
        P(),
        P(None, "wide", "narrow"),
        P("narrow", "wide"),
        P("wide", "narrow"),
    )
    out_specs = (
        P("wide", "narrow"),
        P("wide", "narrow"),
        P("narrow"),
        P(None, "wide", "narrow"),
        P("narrow", "wide"),
        P("narrow"),
        P(None, "wide", "narrow"),
        P("narrow", "wide"),
    )
    return jax.shard_map(shards, mesh=mesh, in_specs=in_specs, out_specs=out_specs, check_vma=False)
```
